512 devices in a mesh: half: 2 (over core), row: 64 (over z, x), col: 4 (over y).
Axes of the slice: x: 4, y: 4, z: 16, core: 2. Of those that a mesh axis runs over, the one named last changes fastest.
Arguments:
- samples: bfloat16 [262144, 512], P(('half', 'row'), 'col'), may hold values from -6 to 6
- couplings: bfloat16 [4096, 64, 512], P(('half', 'row')), may hold values from -0.25 to 0.25
- coupling_cols: int32 [4096, 8], P(('half', 'row')), may hold values from 0 to 4095, as said below
- child_map: int32 [2, 64, 64], P('half', 'row'), may hold values from 0 to 63, each once within a row
- gen_left: bfloat16 [2, 256, 262144], P('half', 'col', 'row'), may hold values from -0.375 to 0.375
- gen_right: bfloat16 [2, 256, 262144], P('half', 'col', 'row'), may hold values from -0.01171875 to 0.01171875
Outputs:
- range_samples: bfloat16 [262144, 512], P(('half', 'row'), 'col')
- row_samples: bfloat16 [262144, 512], P(('half', 'row'), 'col')
The draws below stay inside these ranges and needn't reach their ends.
Inputs may be any that keep to these rules, and one draw needn't show every extreme that they name: `coupling_cols`: slot 0 of block row b is b itself, and every entry lies within 8 blocks of its block row. `child_map`: for each child and row group, the last dimension is a permutation.
All inputs are finite; a program needn't handle non-finite values.
Results may differ from the reference program's by a relative error of at most 0.0075.
Values may be sent and summed in bfloat16 or wider, within the bound.
No kernel may reach another device: no remote copies, remote signals or barrier semaphores. Data moves between devices by JAX's collectives and lax.ppermute only.
A program may use at most 64 MiB of HBM per device.

```python
import jax
import jax.numpy as jnp
from jax import lax

BS = 64
NB = 8
HB = 8
S = 512
K = 256
BLK_DEV = 32
GROUPS = 64
NBK = 4096
NF = 262144
N_HALF = 2
N_ROW = 64


def draw_coupling_cols(key, part):
    block_rows = jnp.arange(NBK, dtype=jnp.int32)[:, None]
    offsets = jax.random.randint(key, (NBK, NB), -HB, HB + 1, dtype=jnp.int32)
    offsets = offsets.at[:, 0].set(0)
    return jnp.clip(block_rows + offsets, 0, NBK - 1).astype(jnp.int32)


def steps_of(rng, extent, split, least, largest):
    factor_of, own = 1.0, jax.random.fold_in(rng, 6)
    for dim, parts in split:
        heights = jnp.exp(jax.random.uniform(jax.random.fold_in(own, dim), (parts,), jnp.float32, least / len(split), largest / len(split)))
        factor_of = factor_of * jnp.repeat(heights, extent[dim] // parts).reshape([-1 if axis == dim else 1 for axis in range(len(extent))])
    return factor_of


def scatter_about(stream_key, dims, scale, reach, split=(), held_as=jnp.bfloat16):
    drawn = scale * jax.random.normal(stream_key, dims, jnp.float32)
    if split:
        drawn = drawn * steps_of(stream_key, dims, split, -0.22, 0.18)
    return jnp.clip(drawn, -reach, reach).astype(held_as)


def setup_inputs(seed: int = 0) -> dict:
    arg_keys = jax.random.split(jax.random.key(seed), 7)
    samples = scatter_about(arg_keys[0], (NF, S), 1.0, 6.0, ((0, 128), (1, 4)))
    couplings = scatter_about(arg_keys[1], (NBK, BS, NB * BS), (NB * BS) ** -0.5, 0.25, ((0, 128),))
    coupling_cols = draw_coupling_cols(jax.random.fold_in(arg_keys[6], 71), 0)
    child_map = jax.vmap(lambda own: jax.random.permutation(own, 2 * BLK_DEV))(jax.random.split(arg_keys[3], N_HALF * GROUPS)).reshape((N_HALF, GROUPS, 2 * BLK_DEV)).astype(jnp.int32)
    gen_left = scatter_about(arg_keys[4], (N_HALF, K, NF), K ** -0.5, 0.375, ((0, 2), (1, 4), (2, 64)))
    gen_right = scatter_about(arg_keys[5], (N_HALF, K, NF), NF ** -0.5, 0.01171875, ((0, 2), (1, 4), (2, 64)))
    return dict(samples=samples, couplings=couplings, coupling_cols=coupling_cols, child_map=child_map, gen_left=gen_left, gen_right=gen_right)


def front_index(order_map):
    piece = 2 * BLK_DEV // N_ROW
    source = order_map // piece
    within = order_map % piece
    slot = jnp.arange(N_ROW, dtype=jnp.int32)[:, None] * piece + within
    half_index = slot // BLK_DEV
    return ((half_index * N_ROW + source) * BLK_DEV + slot % BLK_DEV).reshape(-1).astype(jnp.int32)


def reference(samples, couplings, coupling_cols, child_map, gen_left, gen_right):
    total_blocks = NF // BS
    sample_blocks = samples.reshape(total_blocks, BS, S)
    coupling_groups = couplings.reshape(-1, BLK_DEV, BS, NB * BS)
    col_groups = coupling_cols.reshape(-1, BLK_DEV, NB)
    row_groups = sample_blocks.reshape(-1, BLK_DEV, BS, S)

    def range_group(pair):
        block_rows, block_cols = pair
        gathered = sample_blocks[block_cols].reshape(BLK_DEV, NB * BS, S)
        return jnp.einsum('bik,bks->bis', block_rows.astype(jnp.float32), gathered.astype(jnp.float32))

    sparse_range = lax.map(range_group, (coupling_groups, col_groups)).reshape(NF, S)

    def row_group(total, triple):
        block_rows, block_cols, own_rows = triple
        terms = jnp.einsum('bik,bis->bks', block_rows.astype(jnp.float32), own_rows.astype(jnp.float32))
        terms = terms.reshape(BLK_DEV * NB, BS, S)
        return total.at[block_cols.reshape(-1)].add(terms), None

    sparse_rows, unused = lax.scan(row_group, jnp.zeros((total_blocks, BS, S), jnp.float32),
                                   (coupling_groups, col_groups, row_groups))
    child_range = jnp.zeros((total_blocks, BS, S), jnp.float32)
    child_rows = jnp.zeros((total_blocks, BS, S), jnp.float32)
    for child in range(N_HALF):
        mapping = front_index(child_map[child])
        gathered = sample_blocks[mapping].reshape(NF, S)
        left_gen = gen_left[child]
        right_gen = gen_right[child]
        w_block = jnp.dot(right_gen, gathered, preferred_element_type=jnp.float32).astype(jnp.bfloat16)
        g_block = jnp.dot(left_gen, gathered, preferred_element_type=jnp.float32).astype(jnp.bfloat16)
        range_part = jnp.dot(left_gen.T, w_block, preferred_element_type=jnp.float32).astype(jnp.bfloat16)
        rows_part = jnp.dot(right_gen.T, g_block, preferred_element_type=jnp.float32).astype(jnp.bfloat16)
        range_part = lax.optimization_barrier(range_part).astype(jnp.float32)
        rows_part = lax.optimization_barrier(rows_part).astype(jnp.float32)
        child_range = child_range.at[mapping].add(range_part.reshape(total_blocks, BS, S))
        child_rows = child_rows.at[mapping].add(rows_part.reshape(total_blocks, BS, S))
    range_samples = (sparse_range + child_range.reshape(NF, S)).astype(jnp.bfloat16)
    row_samples = (sparse_rows.reshape(NF, S) + child_rows.reshape(NF, S)).astype(jnp.bfloat16)
    return (range_samples, row_samples)
```

```python
import functools

import jax
import jax.numpy as jnp
from jax import lax
from jax.experimental import pallas as pl
from jax.experimental.pallas import tpu as pltpu
from jax.sharding import Mesh
from jax.sharding import PartitionSpec as P

BS = 64
NB = 8
HB = 8
LANES = 128
CHUNKS = 1
FRONT = ("half", "z", "x")
F32 = jnp.float32
BF16 = jnp.bfloat16
VMEM = pltpu.VMEM
SMEM = pltpu.SMEM


def whole(space):
    return pl.BlockSpec(memory_space=space)


def cost(flops, moved):
    return pl.CostEstimate(flops=flops, bytes_accessed=moved, transcendentals=0)


def swapped_halves(x):
    return pltpu.roll(x.astype(F32), BS, 1).astype(BF16)


def low_lanes(shape):
    return lax.broadcasted_iota(jnp.int32, shape, 1) < BS


def pack_kernel(map_ref, left_ref, right_ref, *out_refs):
    ranks = left_ref.shape[0] // len(out_refs)
    low = low_lanes((ranks, LANES))
    for k in range(left_ref.shape[1] // LANES):
        one, two = map_ref[2 * k], map_ref[2 * k + 1]
        for part, out_ref in enumerate(out_refs):
            rows = slice(part * ranks, (part + 1) * ranks)
            left = left_ref[rows, k * LANES : (k + 1) * LANES]
            right = right_ref[rows, k * LANES : (k + 1) * LANES]
            out_ref[one] = jnp.where(low, left, swapped_halves(right))
            out_ref[two] = jnp.where(low, swapped_halves(left), right)


def pack(order_map, left, right):
    ranks, width = left.shape
    out = jax.ShapeDtypeStruct((width // BS, ranks // CHUNKS, LANES), BF16)
    return pl.pallas_call(
        pack_kernel,
        out_shape=(out,) * CHUNKS,
        in_specs=[whole(SMEM), whole(VMEM), whole(VMEM)],
        out_specs=(whole(VMEM),) * CHUNKS,
        cost_estimate=cost(0, 8 * ranks * width),
        name="pack",
    )(order_map, left, right)


def sparse_kernel(
    cols_ref, a_ref, own_ref, low_ref, high_ref, range_ref, rows_ref, up_ref, down_ref, padded, spread
):
    per = a_ref.shape[0]
    count = own_ref.shape[0]
    step = pl.program_id(0)

    @pl.when(step == 0)
    def _():
        padded[:HB] = low_ref[...]
        padded[HB : HB + count] = own_ref[...]
        padded[HB + count :] = high_ref[...]
        spread[...] = jnp.zeros_like(spread)

    for i in range(per):
        b = step * per + i
        at = [cols_ref[b, t] for t in range(NB)]
        picked = jnp.concatenate([padded[c] for c in at], axis=0)
        a = a_ref[i]
        range_ref[i] = jnp.dot(a, picked, preferred_element_type=F32)
        terms = lax.dot_general(
            a, own_ref[b], (((0,), (0,)), ((), ())), preferred_element_type=F32
        )
        for t in range(NB):
            spread[at[t]] += terms[t * BS : (t + 1) * BS]

    @pl.when(step == pl.num_programs(0) - 1)
    def _():
        rows_ref[...] = spread[HB : HB + count]
        up_ref[...] = spread[HB + count :].astype(BF16)
        down_ref[...] = spread[:HB].astype(BF16)


def sparse(local_cols, couplings, blocks, low, high):
    count, _, width = blocks.shape
    per = 8
    edge = jax.ShapeDtypeStruct((HB, BS, width), BF16)
    return pl.pallas_call(
        sparse_kernel,
        grid=(count // per,),
        out_shape=(
            jax.ShapeDtypeStruct((count, BS, width), F32),
            jax.ShapeDtypeStruct((count, BS, width), F32),
            edge,
            edge,
        ),
        in_specs=[
            whole(SMEM),
            pl.BlockSpec((per, BS, NB * BS), lambda i: (i, 0, 0)),
            whole(VMEM),
            whole(VMEM),
            whole(VMEM),
        ],
        out_specs=(
            pl.BlockSpec((per, BS, width), lambda i: (i, 0, 0)),
            whole(VMEM),
            whole(VMEM),
            whole(VMEM),
        ),
        scratch_shapes=[
            pltpu.VMEM((count + 2 * HB, BS, width), BF16),
            pltpu.VMEM((count + 2 * HB, BS, width), F32),
        ],
        compiler_params=pltpu.CompilerParams(dimension_semantics=("arbitrary",)),
        cost_estimate=cost(4 * count * BS * BS * NB * width, 6 << 20),
        name="sparse",
    )(local_cols, couplings, blocks, low, high)


def reduce_kernel(at_ref, *refs):
    gen_refs, (own_ref, other_ref, out_ref, lhs) = refs[:CHUNKS], refs[CHUNKS:]
    half, me = at_ref[0], at_ref[1]
    blocks, ranks, _ = gen_refs[0].shape
    count = blocks // 2
    parts = own_ref.shape[0]
    low = low_lanes((ranks, LANES))
    for side, first in ((0, half * count), (1, (1 - half) * count)):
        for part, gen_ref in enumerate(gen_refs):
            left = slice(part * ranks, (part + 1) * ranks)
            right = slice((CHUNKS + part) * ranks, (CHUNKS + part + 1) * ranks)
            for k in range(count // 2):
                one, two = gen_ref[first + 2 * k], gen_ref[first + 2 * k + 1]
                lanes = slice(k * LANES, (k + 1) * LANES)
                lhs[side, left, lanes] = jnp.where(low, one, swapped_halves(two))
                lhs[side, right, lanes] = jnp.where(low, swapped_halves(one), two)
    for pair in range(0, parts, 2):
        total = 0.0
        for side, ref in ((0, own_ref), (1, other_ref)):
            rhs = jnp.concatenate([ref[pair], ref[pair + 1]], axis=1)
            total += jnp.dot(lhs[side], rhs, preferred_element_type=F32)
        for k in range(2):
            piece = total[:, k * LANES : (k + 1) * LANES]
            slot = lax.rem(me + parts - (pair + k), parts)
            out_ref[:, slot] = piece.reshape(out_ref.shape[0], -1, LANES).astype(BF16)


def reduced(at, gens, own, other, splits):
    ranks = CHUNKS * gens[0].shape[1]
    parts, rows, _ = own.shape
    return pl.pallas_call(
        reduce_kernel,
        out_shape=jax.ShapeDtypeStruct((splits, parts, 2 * ranks // splits, LANES), BF16),
        in_specs=[whole(SMEM)] + [whole(VMEM)] * (CHUNKS + 2),
        out_specs=whole(VMEM),
        scratch_shapes=[pltpu.VMEM((2, 2 * ranks, rows), BF16)],
        cost_estimate=cost(8 * ranks * rows * parts * LANES, 6 << 20),
        name="partials",
    )(at, *gens, own, other)


def low_rank_kernel(mine, at_ref, own, up, far_a, far_b, down, w_ref, *refs):
    me, step, steps = at_ref[1], pl.program_id(0), pl.num_programs(0)
    per, ranks, _ = own.shape
    rhs = refs[-1]
    parts = rhs.shape[0] // ranks

    @pl.when(step == 0)
    def _():
        for k in range(parts):
            both = w_ref[:, lax.rem(me + parts - k, parts)].reshape(2 * ranks, LANES)
            rows = slice(k * ranks, (k + 1) * ranks)
            rhs[rows, :LANES] = both[ranks:]
            rhs[rows, LANES:] = both[:ranks]

    for i in range(per):
        lhs = jnp.concatenate([g[i] for g in (own, up, far_a, far_b, down)], axis=0)
        both = lax.dot_general(
            lhs, rhs[...], (((0,), (0,)), ((), ())), preferred_element_type=F32
        )
        for_range, for_rows = both[:BS, :LANES], both[BS:, LANES:]
        if mine:
            sr_ref, sp_ref, below_ref, above_ref, out_ref = refs[:-1]
            for_range += sr_ref[i]
            for_rows += sp_ref[i]
            for_rows += jnp.where(step == 0, below_ref[i].astype(F32), 0.0)
            for_rows += jnp.where(step == steps - 1, above_ref[i].astype(F32), 0.0)
        else:
            out_ref = refs[0]
        out_ref[0, i] = for_range.astype(out_ref.dtype)
        out_ref[1, i] = for_rows.astype(out_ref.dtype)


def low_rank(at, gens, w, added=()):
    blocks, ranks, _ = gens[0].shape
    count, per = blocks // 2, HB
    steps = count // per
    mine = bool(added)
    depth = sum(g.shape[1] for g in gens)

    def place(i, at_ref):
        half = at_ref[0] if mine else 1 - at_ref[0]
        return (half * steps + i, 0, 0)

    def tiles(rows):
        return pl.BlockSpec((per, rows, LANES), place)

    edges = [pl.BlockSpec((per, BS, LANES), lambda i, at_ref: (i, 0, 0))] * 2 + [whole(VMEM)] * 2
    return pl.pallas_call(
        functools.partial(low_rank_kernel, mine),
        grid_spec=pltpu.PrefetchScalarGridSpec(
            num_scalar_prefetch=1,
            grid=(steps,),
            in_specs=[tiles(g.shape[1]) for g in gens] + [whole(VMEM)] + (edges if mine else []),
            out_specs=pl.BlockSpec((2, per, BS, LANES), lambda i, at_ref: (0, i, 0, 0)),
            scratch_shapes=[pltpu.VMEM((depth, 2 * LANES), BF16)],
        ),
        out_shape=jax.ShapeDtypeStruct((2, count, BS, LANES), F32 if mine else BF16),
        compiler_params=pltpu.CompilerParams(dimension_semantics=("arbitrary",)),
        cost_estimate=cost(4 * count * LANES * depth * LANES, 4 << 20),
        name="mine" if mine else "theirs",
    )(at, *gens, w, *added)


def around(x, axis, by):
    count = lax.axis_size(axis)
    return lax.ppermute(x, axis, [(i, (i + by) % count) for i in range(count)])


def along_front(x, by):
    count = lax.axis_size(FRONT)
    pairs = [(i, i + by) for i in range(count) if 0 <= i + by < count]
    return lax.ppermute(x, FRONT, pairs)


def spread_out(x, axis):
    return lax.all_to_all(x, axis, split_axis=0, concat_axis=0, tiled=True)


def shards(samples, couplings, coupling_cols, child_map, gen_left, gen_right):
    count = couplings.shape[0]
    width = samples.shape[1]
    half, me = lax.axis_index("half"), lax.axis_index("col")
    at = jnp.stack([half, me]).astype(jnp.int32)
    n_z, n_x, n_col = (lax.axis_size(a) for a in ("z", "x", "col"))
    blocks = samples.reshape(count, BS, width)

    (packed,) = pack(child_map[0, 0], gen_left[0], gen_right[0])
    gens = spread_out(packed, ("z", "x"))

    shifted = [around(samples, "col", k) for k in range(1, n_col)]
    low = along_front(blocks[count - HB :], 1)
    high = along_front(blocks[:HB], -1)
    local_cols = coupling_cols - lax.axis_index(FRONT) * count + HB
    sparse_range, sparse_rows, up, down = sparse(local_cols, couplings, blocks, low, high)
    shifted, up, down = lax.optimization_barrier((shifted, up, down))
    panels = jnp.stack([samples, *shifted])
    others = around(panels, "half", 1)
    below, above = along_front(up, 1), along_front(down, -1)

    gens, panels, others, *added = lax.optimization_barrier(
        (gens, panels, others, sparse_range, sparse_rows, below, above)
    )
    partial = reduced(at, (gens,), panels, others, n_z)
    from_up, from_down = around(gens, "col", 1), around(gens, "col", -1)
    middle = gens.shape[1] // 2
    far_a = around(from_up[:, :middle], "col", 1)
    far_b = around(from_down[:, middle:], "col", -1)

    by_z = jnp.sum(spread_out(partial, "z").astype(F32), axis=0)
    copies = jnp.broadcast_to(by_z, (n_x, *by_z.shape)).reshape(n_x * n_col, *by_z.shape[1:])
    arrived = spread_out(copies, ("x", "col")).reshape(n_x, n_col, *by_z.shape[1:])
    slice_sum = jnp.sum(arrived, axis=0).astype(BF16)
    w = spread_out(jnp.broadcast_to(slice_sum, (n_z, *slice_sum.shape)), "z")

    everyone = (gens, from_up, far_a, far_b, from_down)
    received = around(low_rank(at, everyone, w), "half", 1)
    total = low_rank(at, everyone, w, added) + received.astype(F32)
    range_out, rows_out = total[0].astype(BF16), total[1].astype(BF16)
    return range_out.reshape(samples.shape), rows_out.reshape(samples.shape)


def solution(mesh):
    n_half, n_row, n_col = (mesh.shape[a] for a in ("half", "row", "col"))
    n_x = n_col
    fine = Mesh(
        mesh.devices.reshape(n_half, n_row // n_x, n_x, n_col), ("half", "z", "x", "col")
    )
    row = ("z", "x")
    placed = (
        P(FRONT, "col"),
        P(FRONT, None, None),
        P(FRONT, None),
        P("half", row, None),
        P("half", "col", row),
        P("half", "col", row),
    )
    return jax.shard_map(
        shards,
        mesh=fine,
        in_specs=placed,
        out_specs=(P(FRONT, "col"), P(FRONT, "col")),
        check_vma=False,
    )
```

```python
import functools

import jax
import jax.numpy as jnp
from jax import lax
from jax.experimental import pallas as pl
from jax.experimental.pallas import tpu as pltpu
from jax.sharding import Mesh
from jax.sharding import PartitionSpec as P

BS = 64
NB = 8
HB = 8
LANES = 128
CHUNKS = 1
FRONT = ("half", "z", "x")
F32 = jnp.float32
BF16 = jnp.bfloat16
VMEM = pltpu.VMEM
SMEM = pltpu.SMEM


def whole(space):
    return pl.BlockSpec(memory_space=space)


def cost(flops, moved):
    return pl.CostEstimate(flops=flops, bytes_accessed=moved, transcendentals=0)


def swapped_halves(x):
    return pltpu.roll(x.astype(F32), BS, 1).astype(BF16)


def low_lanes(shape):
    return lax.broadcasted_iota(jnp.int32, shape, 1) < BS


def pack_kernel(map_ref, left_ref, right_ref, *out_refs):
    ranks = left_ref.shape[0] // len(out_refs)
    low = low_lanes((ranks, LANES))
    for k in range(left_ref.shape[1] // LANES):
        one, two = map_ref[2 * k], map_ref[2 * k + 1]
        for part, out_ref in enumerate(out_refs):
            rows = slice(part * ranks, (part + 1) * ranks)
            left = left_ref[rows, k * LANES : (k + 1) * LANES]
            right = right_ref[rows, k * LANES : (k + 1) * LANES]
            out_ref[one] = jnp.where(low, left, swapped_halves(right))
            out_ref[two] = jnp.where(low, swapped_halves(left), right)


def pack(order_map, left, right):
    ranks, width = left.shape
    out = jax.ShapeDtypeStruct((width // BS, ranks // CHUNKS, LANES), BF16)
    return pl.pallas_call(
        pack_kernel,
        out_shape=(out,) * CHUNKS,
        in_specs=[whole(SMEM), whole(VMEM), whole(VMEM)],
        out_specs=(whole(VMEM),) * CHUNKS,
        cost_estimate=cost(0, 8 * ranks * width),
        name="pack",
    )(order_map, left, right)


def sparse_kernel(
    cols_ref, a_ref, own_ref, low_ref, high_ref, range_ref, rows_ref, up_ref, down_ref, padded, spread
):
    per = a_ref.shape[0]
    count = own_ref.shape[0]
    step = pl.program_id(0)

    @pl.when(step == 0)
    def _():
        padded[:HB] = low_ref[...]
        padded[HB : HB + count] = own_ref[...]
        padded[HB + count :] = high_ref[...]
        spread[...] = jnp.zeros_like(spread)

    for i in range(per):
        b = step * per + i
        at = [cols_ref[b, t] for t in range(NB)]
        picked = jnp.concatenate([padded[c] for c in at], axis=0)
        a = a_ref[i]
        range_ref[i] = jnp.dot(a, picked, preferred_element_type=F32)
        terms = lax.dot_general(
            a, own_ref[b], (((0,), (0,)), ((), ())), preferred_element_type=F32
        )
        for t in range(NB):
            spread[at[t]] += terms[t * BS : (t + 1) * BS]

    @pl.when(step == pl.num_programs(0) - 1)
    def _():
        rows_ref[...] = spread[HB : HB + count]
        up_ref[...] = spread[HB + count :].astype(BF16)
        down_ref[...] = spread[:HB].astype(BF16)


def sparse(local_cols, couplings, blocks, low, high):
    count, _, width = blocks.shape
    per = 8
    edge = jax.ShapeDtypeStruct((HB, BS, width), BF16)
    return pl.pallas_call(
        sparse_kernel,
        grid=(count // per,),
        out_shape=(
            jax.ShapeDtypeStruct((count, BS, width), F32),
            jax.ShapeDtypeStruct((count, BS, width), F32),
            edge,
            edge,
        ),
        in_specs=[
            whole(SMEM),
            pl.BlockSpec((per, BS, NB * BS), lambda i: (i, 0, 0)),
            whole(VMEM),
            whole(VMEM),
            whole(VMEM),
        ],
        out_specs=(
            pl.BlockSpec((per, BS, width), lambda i: (i, 0, 0)),
            whole(VMEM),
            whole(VMEM),
            whole(VMEM),
        ),
        scratch_shapes=[
            pltpu.VMEM((count + 2 * HB, BS, width), BF16),
            pltpu.VMEM((count + 2 * HB, BS, width), F32),
        ],
        compiler_params=pltpu.CompilerParams(dimension_semantics=("arbitrary",)),
        cost_estimate=cost(4 * count * BS * BS * NB * width, 6 << 20),
        name="sparse",
    )(local_cols, couplings, blocks, low, high)


def reduce_kernel(at_ref, gen_ref, *refs):
    panels, (out_ref, first_ref, second_ref, lhs) = refs[:-4], refs[-4:]
    half, me = at_ref[0], at_ref[1]
    blocks, ranks, _ = gen_ref.shape
    count = blocks // 2
    parts = len(panels) // 2
    low = low_lanes((ranks, LANES))
    first_ref[...] = gen_ref[:, : ranks // 2]
    second_ref[...] = gen_ref[:, ranks // 2 :]
    for side, first in ((0, half * count), (1, (1 - half) * count)):
        for k in range(count // 2):
            one, two = gen_ref[first + 2 * k], gen_ref[first + 2 * k + 1]
            lanes = slice(k * LANES, (k + 1) * LANES)
            lhs[side, :ranks, lanes] = jnp.where(low, one, swapped_halves(two))
            lhs[side, ranks:, lanes] = jnp.where(low, swapped_halves(one), two)
    for pair in range(0, parts, 2):
        total = 0.0
        for side in range(2):
            ours = panels[side * parts + pair : side * parts + pair + 2]
            rhs = jnp.concatenate([p[0] for p in ours], axis=1)
            total += jnp.dot(lhs[side], rhs, preferred_element_type=F32)
        for k in range(2):
            piece = total[:, k * LANES : (k + 1) * LANES]
            slot = lax.rem(me + parts - (pair + k), parts)
            out_ref[:, slot] = piece.reshape(out_ref.shape[0], -1, LANES).astype(BF16)


def reduced(at, gens, panels, splits):
    blocks, ranks, _ = gens.shape
    rows = blocks * BS // 2
    parts = len(panels) // 2
    half_ranks = jax.ShapeDtypeStruct((blocks, ranks // 2, LANES), BF16)

    def side(p, which):
        which = which if p.shape[0] == 2 else 0
        return pl.BlockSpec((1, rows, LANES), lambda i: (which, 0, 0))

    def same(shape):
        return pl.BlockSpec(shape, lambda i: (0,) * len(shape))

    out = (splits, parts, 2 * ranks // splits, LANES)
    return pl.pallas_call(
        reduce_kernel,
        grid=(1,),
        out_shape=(jax.ShapeDtypeStruct(out, BF16), half_ranks, half_ranks),
        in_specs=[whole(SMEM), same(gens.shape)]
        + [side(p, k // parts) for k, p in enumerate(panels)],
        out_specs=(same(out), same(half_ranks.shape), same(half_ranks.shape)),
        scratch_shapes=[pltpu.VMEM((2, 2 * ranks, rows), BF16)],
        cost_estimate=cost(8 * ranks * rows * parts * LANES, 6 << 20),
        name="partials",
    )(at, gens, *panels)


def low_rank_kernel(mine, pieces, at_ref, *refs):
    gens, w_ref, refs = refs[:pieces], refs[pieces], refs[pieces + 1 :]
    own = gens[0]
    me, step, steps = at_ref[1], pl.program_id(0), pl.num_programs(0)
    per, ranks, _ = own.shape
    rhs = refs[-1]
    parts = rhs.shape[0] // ranks

    @pl.when(step == 0)
    def _():
        for k in range(parts):
            both = w_ref[:, lax.rem(me + parts - k, parts)].reshape(2 * ranks, LANES)
            rows = slice(k * ranks, (k + 1) * ranks)
            rhs[rows, :LANES] = both[ranks:]
            rhs[rows, LANES:] = both[:ranks]

    for i in range(per):
        lhs = jnp.concatenate([g[i] for g in gens], axis=0)
        both = lax.dot_general(
            lhs, rhs[...], (((0,), (0,)), ((), ())), preferred_element_type=F32
        )
        for_range, for_rows = both[:BS, :LANES], both[BS:, LANES:]
        if mine:
            sr_ref, sp_ref, below_ref, above_ref, out_ref = refs[:-1]
            for_range += sr_ref[i]
            for_rows += sp_ref[i]
            for_rows += jnp.where(step == 0, below_ref[i].astype(F32), 0.0)
            for_rows += jnp.where(step == steps - 1, above_ref[i].astype(F32), 0.0)
        else:
            out_ref = refs[0]
        out_ref[0, i] = for_range.astype(out_ref.dtype)
        out_ref[1, i] = for_rows.astype(out_ref.dtype)


def low_rank(at, gens, w, added=()):
    blocks, _, _ = gens[0].shape
    count, per = blocks // 2, HB
    steps = count // per
    mine = bool(added)
    depth = sum(g.shape[1] for g in gens)

    def place(i, at_ref):
        half = at_ref[0] if mine else 1 - at_ref[0]
        return (half * steps + i, 0, 0)

    def tiles(rows):
        return pl.BlockSpec((per, rows, LANES), place)

    edges = [pl.BlockSpec((per, BS, LANES), lambda i, at_ref: (i, 0, 0))] * 2 + [whole(VMEM)] * 2
    return pl.pallas_call(
        functools.partial(low_rank_kernel, mine, len(gens)),
        grid_spec=pltpu.PrefetchScalarGridSpec(
            num_scalar_prefetch=1,
            grid=(steps,),
            in_specs=[tiles(g.shape[1]) for g in gens] + [whole(VMEM)] + (edges if mine else []),
            out_specs=pl.BlockSpec((2, per, BS, LANES), lambda i, at_ref: (0, i, 0, 0)),
            scratch_shapes=[pltpu.VMEM((depth, 2 * LANES), BF16)],
        ),
        out_shape=jax.ShapeDtypeStruct((2, count, BS, LANES), F32 if mine else BF16),
        compiler_params=pltpu.CompilerParams(dimension_semantics=("arbitrary",)),
        cost_estimate=cost(4 * count * LANES * depth * LANES, 4 << 20),
        name="mine" if mine else "theirs",
    )(at, *gens, w, *added)


def around(x, axis, by):
    count = lax.axis_size(axis)
    return lax.ppermute(x, axis, [(i, (i + by) % count) for i in range(count)])


def along_front(x, by):
    count = lax.axis_size(FRONT)
    pairs = [(i, i + by) for i in range(count) if 0 <= i + by < count]
    return lax.ppermute(x, FRONT, pairs)


def spread_out(x, axis):
    return lax.all_to_all(x, axis, split_axis=0, concat_axis=0, tiled=True)


def shards(samples, couplings, coupling_cols, child_map, gen_left, gen_right):
    count = couplings.shape[0]
    width = samples.shape[1]
    half, me = lax.axis_index("half"), lax.axis_index("col")
    at = jnp.stack([half, me]).astype(jnp.int32)
    n_z, n_x, n_col = (lax.axis_size(a) for a in ("z", "x", "col"))
    blocks = samples.reshape(count, BS, width)

    low = along_front(blocks[count - HB :], 1)
    high = along_front(blocks[:HB], -1)
    other = around(samples, "half", 1)
    (packed,) = pack(child_map[0, 0], gen_left[0], gen_right[0])
    gens = spread_out(packed, ("z", "x"))

    both = jnp.stack([samples, other])
    s_up, s_down = around(both, "col", 1), around(both, "col", -1)
    local_cols = coupling_cols - lax.axis_index(FRONT) * count + HB
    sparse_range, sparse_rows, up, down = sparse(local_cols, couplings, blocks, low, high)
    s_up, s_down, up, down = lax.optimization_barrier((s_up, s_down, up, down))
    s_far, o_far = around(s_up[:1], "col", 1), around(s_down[1:], "col", -1)
    below, above = along_front(up, 1), along_front(down, -1)
    panels = (both, s_up, s_far, s_down, both, s_up, o_far, s_down)

    gens, panels, sparse_range, sparse_rows = lax.optimization_barrier(
        (gens, panels, sparse_range, sparse_rows)
    )
    added = (sparse_range, sparse_rows, below, above)
    partial, first, second = reduced(at, gens, panels, n_z)
    up_a, down_b = around(first, "col", 1), around(second, "col", -1)
    up_b, down_a = around(second, "col", 1), around(first, "col", -1)
    far_a, far_b = around(up_a, "col", 1), around(down_b, "col", -1)

    by_z = spread_out(partial, "z")
    by_z = jnp.sum(by_z.astype(F32), axis=0)
    copies = jnp.broadcast_to(by_z, (n_x, *by_z.shape)).reshape(n_x * n_col, *by_z.shape[1:])
    arrived = spread_out(copies, ("x", "col"))
    slice_sum = jnp.sum(arrived.reshape(n_x, n_col, *by_z.shape[1:]), axis=0).astype(BF16)
    copies = jnp.broadcast_to(slice_sum, (n_z, *slice_sum.shape))
    w = spread_out(copies, "z")

    everyone = (gens, up_a, up_b, far_a, far_b, down_a, down_b)
    received = around(low_rank(at, everyone, w), "half", 1)
    total = low_rank(at, everyone, w, added) + received.astype(F32)
    range_out, rows_out = total[0].astype(BF16), total[1].astype(BF16)
    return range_out.reshape(samples.shape), rows_out.reshape(samples.shape)


def solution(mesh):
    n_half, n_row, n_col = (mesh.shape[a] for a in ("half", "row", "col"))
    n_x = n_col
    fine = Mesh(
        mesh.devices.reshape(n_half, n_row // n_x, n_x, n_col), ("half", "z", "x", "col")
    )
    row = ("z", "x")
    placed = (
        P(FRONT, "col"),
        P(FRONT, None, None),
        P(FRONT, None),
        P("half", row, None),
        P("half", "col", row),
        P("half", "col", row),
    )
    return jax.shard_map(
        shards,
        mesh=fine,
        in_specs=placed,
        out_specs=(P(FRONT, "col"), P(FRONT, "col")),
        check_vma=False,
    )
```

```python
import functools

import jax
import jax.numpy as jnp
from jax import lax
from jax.experimental import pallas as pl
from jax.experimental.pallas import tpu as pltpu
from jax.sharding import Mesh
from jax.sharding import PartitionSpec as P

BS = 64
NB = 8
HB = 8
LANES = 128
CHUNKS = 1
FRONT = ("half", "z", "x")
F32 = jnp.float32
BF16 = jnp.bfloat16
VMEM = pltpu.VMEM
SMEM = pltpu.SMEM


def whole(space):
    return pl.BlockSpec(memory_space=space)


def cost(flops, moved):
    return pl.CostEstimate(flops=flops, bytes_accessed=moved, transcendentals=0)


def swapped_halves(x):
    return pltpu.roll(x.astype(F32), BS, 1).astype(BF16)


def low_lanes(shape):
    return lax.broadcasted_iota(jnp.int32, shape, 1) < BS


def pack_kernel(map_ref, left_ref, right_ref, *out_refs):
    ranks = left_ref.shape[0] // len(out_refs)
    low = low_lanes((ranks, LANES))
    for k in range(left_ref.shape[1] // LANES):
        one, two = map_ref[2 * k], map_ref[2 * k + 1]
        for part, out_ref in enumerate(out_refs):
            rows = slice(part * ranks, (part + 1) * ranks)
            left = left_ref[rows, k * LANES : (k + 1) * LANES]
            right = right_ref[rows, k * LANES : (k + 1) * LANES]
            out_ref[one] = jnp.where(low, left, swapped_halves(right))
            out_ref[two] = jnp.where(low, swapped_halves(left), right)


def pack(order_map, left, right):
    ranks, width = left.shape
    out = jax.ShapeDtypeStruct((width // BS, ranks // CHUNKS, LANES), BF16)
    return pl.pallas_call(
        pack_kernel,
        out_shape=(out,) * CHUNKS,
        in_specs=[whole(SMEM), whole(VMEM), whole(VMEM)],
        out_specs=(whole(VMEM),) * CHUNKS,
        cost_estimate=cost(0, 8 * ranks * width),
        name="pack",
    )(order_map, left, right)


def sparse_kernel(
    cols_ref, a_ref, own_ref, low_ref, high_ref, range_ref, rows_ref, up_ref, down_ref, padded, spread
):
    per = a_ref.shape[0]
    count = own_ref.shape[0]
    step = pl.program_id(0)

    @pl.when(step == 0)
    def _():
        padded[:HB] = low_ref[...]
        padded[HB : HB + count] = own_ref[...]
        padded[HB + count :] = high_ref[...]
        spread[...] = jnp.zeros_like(spread)

    for i in range(per):
        b = step * per + i
        at = [cols_ref[b, t] for t in range(NB)]
        picked = jnp.concatenate([padded[c] for c in at], axis=0)
        a = a_ref[i]
        range_ref[i] = jnp.dot(a, picked, preferred_element_type=F32)
        terms = lax.dot_general(
            a, own_ref[b], (((0,), (0,)), ((), ())), preferred_element_type=F32
        )
        for t in range(NB):
            spread[at[t]] += terms[t * BS : (t + 1) * BS]

    @pl.when(step == pl.num_programs(0) - 1)
    def _():
        rows_ref[...] = spread[HB : HB + count]
        up_ref[...] = spread[HB + count :].astype(BF16)
        down_ref[...] = spread[:HB].astype(BF16)


def sparse(local_cols, couplings, blocks, low, high):
    count, _, width = blocks.shape
    per = 8
    edge = jax.ShapeDtypeStruct((HB, BS, width), BF16)
    return pl.pallas_call(
        sparse_kernel,
        grid=(count // per,),
        out_shape=(
            jax.ShapeDtypeStruct((count, BS, width), F32),
            jax.ShapeDtypeStruct((count, BS, width), F32),
            edge,
            edge,
        ),
        in_specs=[
            whole(SMEM),
            pl.BlockSpec((per, BS, NB * BS), lambda i: (i, 0, 0)),
            whole(VMEM),
            whole(VMEM),
            whole(VMEM),
        ],
        out_specs=(
            pl.BlockSpec((per, BS, width), lambda i: (i, 0, 0)),
            whole(VMEM),
            whole(VMEM),
            whole(VMEM),
        ),
        scratch_shapes=[
            pltpu.VMEM((count + 2 * HB, BS, width), BF16),
            pltpu.VMEM((count + 2 * HB, BS, width), F32),
        ],
        compiler_params=pltpu.CompilerParams(dimension_semantics=("arbitrary",)),
        cost_estimate=cost(4 * count * BS * BS * NB * width, 6 << 20),
        name="sparse",
    )(local_cols, couplings, blocks, low, high)


def reduce_kernel(at_ref, gen_ref, own_ref, other_ref, out_ref, first_ref, second_ref, lhs):
    half, me = at_ref[0], at_ref[1]
    blocks, ranks, _ = gen_ref.shape
    count = blocks // 2
    parts = own_ref.shape[0]
    low = low_lanes((ranks, LANES))
    first_ref[...] = gen_ref[:, : ranks // 2]
    second_ref[...] = gen_ref[:, ranks // 2 :]
    for side, first in ((0, half * count), (1, (1 - half) * count)):
        for k in range(count // 2):
            one, two = gen_ref[first + 2 * k], gen_ref[first + 2 * k + 1]
            lanes = slice(k * LANES, (k + 1) * LANES)
            lhs[side, :ranks, lanes] = jnp.where(low, one, swapped_halves(two))
            lhs[side, ranks:, lanes] = jnp.where(low, swapped_halves(one), two)
    for pair in range(0, parts, 2):
        total = 0.0
        for side, ref in ((0, own_ref), (1, other_ref)):
            rhs = jnp.concatenate([ref[pair], ref[pair + 1]], axis=1)
            total += jnp.dot(lhs[side], rhs, preferred_element_type=F32)
        for k in range(2):
            piece = total[:, k * LANES : (k + 1) * LANES]
            slot = lax.rem(me + parts - (pair + k), parts)
            out_ref[:, slot] = piece.reshape(out_ref.shape[0], -1, LANES).astype(BF16)


def reduced(at, gens, own, other, splits):
    blocks, ranks, _ = gens.shape
    parts, rows, _ = own.shape
    half_ranks = jax.ShapeDtypeStruct((blocks, ranks // 2, LANES), BF16)
    out = jax.ShapeDtypeStruct((splits, parts, 2 * ranks // splits, LANES), BF16)
    return pl.pallas_call(
        reduce_kernel,
        out_shape=(out, half_ranks, half_ranks),
        in_specs=[whole(SMEM)] + [whole(VMEM)] * 3,
        out_specs=(whole(VMEM),) * 3,
        scratch_shapes=[pltpu.VMEM((2, 2 * ranks, rows), BF16)],
        cost_estimate=cost(8 * ranks * rows * parts * LANES, 6 << 20),
        name="partials",
    )(at, gens, own, other)


def low_rank_kernel(mine, pieces, at_ref, *refs):
    gens, w_ref, refs = refs[:pieces], refs[pieces], refs[pieces + 1 :]
    me, step, steps = at_ref[1], pl.program_id(0), pl.num_programs(0)
    per, ranks, _ = gens[0].shape
    lhs = refs[-1]
    parts = lhs.shape[1] // ranks
    low = low_lanes((LANES, LANES))

    @pl.when(step == 0)
    def _():
        for k in range(parts):
            both = w_ref[:, lax.rem(me + parts - k, parts)].reshape(2 * ranks, LANES)
            turned = both.astype(F32).T.astype(BF16)
            lanes = slice(k * ranks, (k + 1) * ranks)
            lhs[:LANES, lanes] = turned[:, ranks:]
            lhs[LANES:, lanes] = turned[:, :ranks]

    for i in range(0, per, 2):
        rhs = jnp.concatenate(
            [jnp.concatenate([g[i + j] for g in gens], axis=0) for j in range(2)], axis=1
        )
        both = jnp.dot(lhs[...], rhs, preferred_element_type=F32)
        for j in range(2):
            lanes = slice(j * LANES, (j + 1) * LANES)
            out = jnp.where(low, both[:LANES, lanes], both[LANES:, lanes]).T
            for_range, for_rows = out[:BS], out[BS:]
            b = i + j
            if mine:
                sr_ref, sp_ref, below_ref, above_ref, range_ref, rows_ref = refs[:-1]
                range_ref[b] = for_range + sr_ref[b]
                for_rows += sp_ref[b]
                for_rows += jnp.where(step == 0, below_ref[b].astype(F32), 0.0)
                for_rows += jnp.where(step == steps - 1, above_ref[b].astype(F32), 0.0)
                rows_ref[b] = for_rows
            else:
                refs[0][0, b] = for_range.astype(BF16)
                refs[0][1, b] = for_rows.astype(BF16)


def low_rank(at, gens, w, added=()):
    blocks, _, _ = gens[0].shape
    count, per = blocks // 2, HB
    steps = count // per
    mine = bool(added)
    depth = sum(g.shape[1] for g in gens)

    def place(i, at_ref):
        half = at_ref[0] if mine else 1 - at_ref[0]
        return (half * steps + i, 0, 0)

    def tiles(rows):
        return pl.BlockSpec((per, rows, LANES), place)

    flat = pl.BlockSpec((per, BS, LANES), lambda i, at_ref: (i, 0, 0))
    edges = [flat] * 2 + [whole(VMEM)] * 2
    if mine:
        out_shape = (jax.ShapeDtypeStruct((count, BS, LANES), F32),) * 2
        out_specs = (flat, flat)
    else:
        out_shape = jax.ShapeDtypeStruct((2, count, BS, LANES), BF16)
        out_specs = pl.BlockSpec((2, per, BS, LANES), lambda i, at_ref: (0, i, 0, 0))
    return pl.pallas_call(
        functools.partial(low_rank_kernel, mine, len(gens)),
        grid_spec=pltpu.PrefetchScalarGridSpec(
            num_scalar_prefetch=1,
            grid=(steps,),
            in_specs=[tiles(g.shape[1]) for g in gens] + [whole(VMEM)] + (edges if mine else []),
            out_specs=out_specs,
            scratch_shapes=[pltpu.VMEM((2 * LANES, depth), BF16)],
        ),
        out_shape=out_shape,
        compiler_params=pltpu.CompilerParams(dimension_semantics=("arbitrary",)),
        cost_estimate=cost(4 * count * LANES * depth * LANES, 4 << 20),
        name="mine" if mine else "theirs",
    )(at, *gens, w, *added)


def around(x, axis, by):
    count = lax.axis_size(axis)
    return lax.ppermute(x, axis, [(i, (i + by) % count) for i in range(count)])


def along_front(x, by):
    count = lax.axis_size(FRONT)
    pairs = [(i, i + by) for i in range(count) if 0 <= i + by < count]
    return lax.ppermute(x, FRONT, pairs)


def spread_out(x, axis):
    return lax.all_to_all(x, axis, split_axis=0, concat_axis=0, tiled=True)


def shards(samples, couplings, coupling_cols, child_map, gen_left, gen_right):
    count = couplings.shape[0]
    width = samples.shape[1]
    half, me = lax.axis_index("half"), lax.axis_index("col")
    at = jnp.stack([half, me]).astype(jnp.int32)
    n_z, n_x, n_col = (lax.axis_size(a) for a in ("z", "x", "col"))
    blocks = samples.reshape(count, BS, width)

    low = along_front(blocks[count - HB :], 1)
    high = along_front(blocks[:HB], -1)
    (packed,) = pack(child_map[0, 0], gen_left[0], gen_right[0])
    gens = spread_out(packed, ("z", "x"))

    shifted = [around(samples, "col", k) for k in range(1, n_col)]
    local_cols = coupling_cols - lax.axis_index(FRONT) * count + HB
    sparse_range, sparse_rows, up, down = sparse(local_cols, couplings, blocks, low, high)
    shifted, up, down = lax.optimization_barrier((shifted, up, down))
    panels = jnp.stack([samples, *shifted])
    others = around(panels, "half", 1)
    below, above = along_front(up, 1), along_front(down, -1)

    gens, panels, others, sparse_range, sparse_rows = lax.optimization_barrier(
        (gens, panels, others, sparse_range, sparse_rows)
    )
    added = (sparse_range, sparse_rows, below, above)
    partial, first, second = reduced(at, gens, panels, others, n_z)
    up_a, down_b = around(first, "col", 1), around(second, "col", -1)
    up_b, down_a = around(second, "col", 1), around(first, "col", -1)
    far_a, far_b = around(up_a, "col", 1), around(down_b, "col", -1)

    by_z = spread_out(partial, "z")
    by_z = jnp.sum(by_z.astype(F32), axis=0)
    copies = jnp.broadcast_to(by_z, (n_x, *by_z.shape)).reshape(n_x * n_col, *by_z.shape[1:])
    arrived = spread_out(copies, ("x", "col"))
    slice_sum = jnp.sum(arrived.reshape(n_x, n_col, *by_z.shape[1:]), axis=0).astype(BF16)
    copies = jnp.broadcast_to(slice_sum, (n_z, *slice_sum.shape))
    w = spread_out(copies, "z")

    everyone = (gens, up_a, up_b, far_a, far_b, down_a, down_b)
    received = around(low_rank(at, everyone, w), "half", 1)
    range_out, rows_out = (
        (ours + theirs.astype(F32)).astype(BF16)
        for ours, theirs in zip(low_rank(at, everyone, w, added), received)
    )
    return range_out.reshape(samples.shape), rows_out.reshape(samples.shape)


def solution(mesh):
    n_half, n_row, n_col = (mesh.shape[a] for a in ("half", "row", "col"))
    n_x = n_col
    fine = Mesh(
        mesh.devices.reshape(n_half, n_row // n_x, n_x, n_col), ("half", "z", "x", "col")
    )
    row = ("z", "x")
    placed = (
        P(FRONT, "col"),
        P(FRONT, None, None),
        P(FRONT, None),
        P("half", row, None),
        P("half", "col", row),
        P("half", "col", row),
    )
    return jax.shard_map(
        shards,
        mesh=fine,
        in_specs=placed,
        out_specs=(P(FRONT, "col"), P(FRONT, "col")),
        check_vma=False,
    )
```

```python
import functools

import jax
import jax.numpy as jnp
from jax import lax
from jax.experimental import pallas as pl
from jax.experimental.pallas import tpu as pltpu
from jax.sharding import Mesh
from jax.sharding import PartitionSpec as P

BS = 64
NB = 8
HB = 8
LANES = 128
CHUNKS = 1
FRONT = ("half", "z", "x")
F32 = jnp.float32
BF16 = jnp.bfloat16
VMEM = pltpu.VMEM
SMEM = pltpu.SMEM


def whole(space):
    return pl.BlockSpec(memory_space=space)


def cost(flops, moved):
    return pl.CostEstimate(flops=flops, bytes_accessed=moved, transcendentals=0)


def grant(mib, **more):
    return pltpu.CompilerParams(vmem_limit_bytes=mib << 20, **more)


def swapped_halves(x):
    return pltpu.roll(x.astype(F32), BS, 1).astype(BF16)


def low_lanes(shape):
    return lax.broadcasted_iota(jnp.int32, shape, 1) < BS


def pack_kernel(map_ref, left_ref, right_ref, *out_refs):
    ranks = left_ref.shape[0] // len(out_refs)
    low = low_lanes((ranks, LANES))
    for k in range(left_ref.shape[1] // LANES):
        one, two = map_ref[2 * k], map_ref[2 * k + 1]
        for part, out_ref in enumerate(out_refs):
            rows = slice(part * ranks, (part + 1) * ranks)
            left = left_ref[rows, k * LANES : (k + 1) * LANES]
            right = right_ref[rows, k * LANES : (k + 1) * LANES]
            out_ref[one] = jnp.where(low, left, swapped_halves(right))
            out_ref[two] = jnp.where(low, swapped_halves(left), right)


def pack(order_map, left, right):
    ranks, width = left.shape
    out = jax.ShapeDtypeStruct((width // BS, ranks // CHUNKS, LANES), BF16)
    return pl.pallas_call(
        pack_kernel,
        out_shape=(out,) * CHUNKS,
        in_specs=[whole(SMEM), whole(VMEM), whole(VMEM)],
        out_specs=(whole(VMEM),) * CHUNKS,
        compiler_params=grant(6),
        cost_estimate=cost(0, 8 * ranks * width),
        name="pack",
    )(order_map, left, right)


def sparse_kernel(
    cols_ref, a_ref, own_ref, low_ref, high_ref, range_ref, rows_ref, up_ref, down_ref, padded, spread
):
    per = a_ref.shape[0]
    count = own_ref.shape[0]
    step = pl.program_id(0)

    @pl.when(step == 0)
    def _():
        padded[:HB] = low_ref[...]
        padded[HB : HB + count] = own_ref[...]
        padded[HB + count :] = high_ref[...]
        spread[...] = jnp.zeros_like(spread)

    for i in range(per):
        b = step * per + i
        at = [cols_ref[b, t] for t in range(NB)]
        picked = jnp.concatenate([padded[c] for c in at], axis=0)
        a = a_ref[i]
        range_ref[i] = jnp.dot(a, picked, preferred_element_type=F32)
        terms = lax.dot_general(
            a, own_ref[b], (((0,), (0,)), ((), ())), preferred_element_type=F32
        )
        for t in range(NB):
            spread[at[t]] += terms[t * BS : (t + 1) * BS]

    @pl.when(step == pl.num_programs(0) - 1)
    def _():
        rows_ref[...] = spread[HB : HB + count]
        up_ref[...] = spread[HB + count :].astype(BF16)
        down_ref[...] = spread[:HB].astype(BF16)


def sparse(local_cols, couplings, blocks, low, high):
    count, _, width = blocks.shape
    per = 8
    edge = jax.ShapeDtypeStruct((HB, BS, width), BF16)
    return pl.pallas_call(
        sparse_kernel,
        grid=(count // per,),
        out_shape=(
            jax.ShapeDtypeStruct((count, BS, width), F32),
            jax.ShapeDtypeStruct((count, BS, width), F32),
            edge,
            edge,
        ),
        in_specs=[
            whole(SMEM),
            pl.BlockSpec((per, BS, NB * BS), lambda i: (i, 0, 0)),
            whole(VMEM),
            whole(VMEM),
            whole(VMEM),
        ],
        out_specs=(
            pl.BlockSpec((per, BS, width), lambda i: (i, 0, 0)),
            whole(VMEM),
            whole(VMEM),
            whole(VMEM),
        ),
        scratch_shapes=[
            pltpu.VMEM((count + 2 * HB, BS, width), BF16),
            pltpu.VMEM((count + 2 * HB, BS, width), F32),
        ],
        compiler_params=grant(12, dimension_semantics=("arbitrary",)),
        cost_estimate=cost(4 * count * BS * BS * NB * width, 6 << 20),
        name="sparse",
    )(local_cols, couplings, blocks, low, high)


def reduce_kernel(at_ref, gen_ref, own_ref, other_ref, out_ref, first_ref, second_ref, lhs):
    half, me = at_ref[0], at_ref[1]
    blocks, ranks, _ = gen_ref.shape
    count = blocks // 2
    parts = own_ref.shape[0]
    low = low_lanes((ranks, LANES))
    first_ref[...] = gen_ref[:, : ranks // 2]
    second_ref[...] = gen_ref[:, ranks // 2 :]
    for side, first in ((0, half * count), (1, (1 - half) * count)):
        for k in range(count // 2):
            one, two = gen_ref[first + 2 * k], gen_ref[first + 2 * k + 1]
            lanes = slice(k * LANES, (k + 1) * LANES)
            lhs[side, :ranks, lanes] = jnp.where(low, one, swapped_halves(two))
            lhs[side, ranks:, lanes] = jnp.where(low, swapped_halves(one), two)
    for pair in range(0, parts, 2):
        total = 0.0
        for side, ref in ((0, own_ref), (1, other_ref)):
            rhs = jnp.concatenate([ref[pair], ref[pair + 1]], axis=1)
            total += jnp.dot(lhs[side], rhs, preferred_element_type=F32)
        for k in range(2):
            piece = total[:, k * LANES : (k + 1) * LANES]
            slot = lax.rem(me + parts - (pair + k), parts)
            out_ref[:, slot] = piece.reshape(out_ref.shape[0], -1, LANES).astype(BF16)


def reduced(at, gens, own, other, splits):
    blocks, ranks, _ = gens.shape
    parts, rows, _ = own.shape
    half_ranks = jax.ShapeDtypeStruct((blocks, ranks // 2, LANES), BF16)
    out = jax.ShapeDtypeStruct((splits, parts, 2 * ranks // splits, LANES), BF16)
    return pl.pallas_call(
        reduce_kernel,
        out_shape=(out, half_ranks, half_ranks),
        in_specs=[whole(SMEM)] + [whole(VMEM)] * 3,
        out_specs=(whole(VMEM),) * 3,
        scratch_shapes=[pltpu.VMEM((2, 2 * ranks, rows), BF16)],
        compiler_params=grant(14),
        cost_estimate=cost(8 * ranks * rows * parts * LANES, 6 << 20),
        name="partials",
    )(at, gens, own, other)


def low_rank_kernel(mine, pieces, at_ref, *refs):
    gens, w_ref, refs = refs[:pieces], refs[pieces], refs[pieces + 1 :]
    me, step, steps = at_ref[1], pl.program_id(0), pl.num_programs(0)
    per, ranks, _ = gens[0].shape
    lhs = refs[-1]
    parts = lhs.shape[1] // ranks
    low = low_lanes((LANES, LANES))

    @pl.when(step == 0)
    def _():
        for k in range(parts):
            both = w_ref[:, lax.rem(me + parts - k, parts)].reshape(2 * ranks, LANES)
            turned = both.astype(F32).T.astype(BF16)
            lanes = slice(k * ranks, (k + 1) * ranks)
            lhs[:LANES, lanes] = turned[:, ranks:]
            lhs[LANES:, lanes] = turned[:, :ranks]

    for i in range(0, per, 2):
        rhs = jnp.concatenate(
            [jnp.concatenate([g[i + j] for g in gens], axis=0) for j in range(2)], axis=1
        )
        both = jnp.dot(lhs[...], rhs, preferred_element_type=F32)
        for j in range(2):
            lanes = slice(j * LANES, (j + 1) * LANES)
            out = jnp.where(low, both[:LANES, lanes], both[LANES:, lanes]).T
            for_range, for_rows = out[:BS], out[BS:]
            b = i + j
            if mine:
                sr_ref, sp_ref, below_ref, above_ref, range_ref, rows_ref = refs[:-1]
                range_ref[b] = for_range + sr_ref[b]
                for_rows += sp_ref[b]
                for_rows += jnp.where(step == 0, below_ref[b].astype(F32), 0.0)
                for_rows += jnp.where(step == steps - 1, above_ref[b].astype(F32), 0.0)
                rows_ref[b] = for_rows
            else:
                refs[0][0, b] = for_range.astype(BF16)
                refs[0][1, b] = for_rows.astype(BF16)


def low_rank(at, gens, w, added=()):
    blocks, _, _ = gens[0].shape
    count, per = blocks // 2, HB
    steps = count // per
    mine = bool(added)
    depth = sum(g.shape[1] for g in gens)

    def place(i, at_ref):
        half = at_ref[0] if mine else 1 - at_ref[0]
        return (half * steps + i, 0, 0)

    def tiles(rows):
        return pl.BlockSpec((per, rows, LANES), place)

    flat = pl.BlockSpec((per, BS, LANES), lambda i, at_ref: (i, 0, 0))
    edges = [flat] * 2 + [whole(VMEM)] * 2
    if mine:
        out_shape = (jax.ShapeDtypeStruct((count, BS, LANES), F32),) * 2
        out_specs = (flat, flat)
    else:
        out_shape = jax.ShapeDtypeStruct((2, count, BS, LANES), BF16)
        out_specs = pl.BlockSpec((2, per, BS, LANES), lambda i, at_ref: (0, i, 0, 0))
    return pl.pallas_call(
        functools.partial(low_rank_kernel, mine, len(gens)),
        grid_spec=pltpu.PrefetchScalarGridSpec(
            num_scalar_prefetch=1,
            grid=(steps,),
            in_specs=[tiles(g.shape[1]) for g in gens] + [whole(VMEM)] + (edges if mine else []),
            out_specs=out_specs,
            scratch_shapes=[pltpu.VMEM((2 * LANES, depth), BF16)],
        ),
        out_shape=out_shape,
        compiler_params=grant(10, dimension_semantics=("arbitrary",)),
        cost_estimate=cost(4 * count * LANES * depth * LANES, 4 << 20),
        name="mine" if mine else "theirs",
    )(at, *gens, w, *added)


def around(x, axis, by):
    count = lax.axis_size(axis)
    return lax.ppermute(x, axis, [(i, (i + by) % count) for i in range(count)])


def along_front(x, by):
    count = lax.axis_size(FRONT)
    pairs = [(i, i + by) for i in range(count) if 0 <= i + by < count]
    return lax.ppermute(x, FRONT, pairs)


def spread_out(x, axis):
    return lax.all_to_all(x, axis, split_axis=0, concat_axis=0, tiled=True)


def shards(samples, couplings, coupling_cols, child_map, gen_left, gen_right):
    count = couplings.shape[0]
    width = samples.shape[1]
    half, me = lax.axis_index("half"), lax.axis_index("col")
    at = jnp.stack([half, me]).astype(jnp.int32)
    n_z, n_x, n_col = (lax.axis_size(a) for a in ("z", "x", "col"))
    blocks = samples.reshape(count, BS, width)

    low = along_front(blocks[count - HB :], 1)
    high = along_front(blocks[:HB], -1)
    (packed,) = pack(child_map[0, 0], gen_left[0], gen_right[0])
    gens = spread_out(packed, ("z", "x"))

    shifted = [around(samples, "col", k) for k in range(1, n_col)]
    local_cols = coupling_cols - lax.axis_index(FRONT) * count + HB
    sparse_range, sparse_rows, up, down = sparse(local_cols, couplings, blocks, low, high)
    shifted, up, down = lax.optimization_barrier((shifted, up, down))
    panels = jnp.stack([samples, *shifted])
    others = around(panels, "half", 1)
    below, above = along_front(up, 1), along_front(down, -1)

    gens, panels, others, sparse_range, sparse_rows = lax.optimization_barrier(
        (gens, panels, others, sparse_range, sparse_rows)
    )
    added = (sparse_range, sparse_rows, below, above)
    partial, first, second = reduced(at, gens, panels, others, n_z)
    up_a, down_b = around(first, "col", 1), around(second, "col", -1)
    up_b, down_a = around(second, "col", 1), around(first, "col", -1)
    far_a, far_b = around(up_a, "col", 1), around(down_b, "col", -1)

    by_z = spread_out(partial, "z")
    by_z = jnp.sum(by_z.astype(F32), axis=0)
    copies = jnp.broadcast_to(by_z, (n_x, *by_z.shape)).reshape(n_x * n_col, *by_z.shape[1:])
    arrived = spread_out(copies, ("x", "col"))
    slice_sum = jnp.sum(arrived.reshape(n_x, n_col, *by_z.shape[1:]), axis=0).astype(BF16)
    copies = jnp.broadcast_to(slice_sum, (n_z, *slice_sum.shape))
    w = spread_out(copies, "z")

    everyone = (gens, up_a, up_b, far_a, far_b, down_a, down_b)
    received = around(low_rank(at, everyone, w), "half", 1)
    range_out, rows_out = (
        (ours + theirs.astype(F32)).astype(BF16)
        for ours, theirs in zip(low_rank(at, everyone, w, added), received)
    )
    return range_out.reshape(samples.shape), rows_out.reshape(samples.shape)


def solution(mesh):
    n_half, n_row, n_col = (mesh.shape[a] for a in ("half", "row", "col"))
    n_x = n_col
    fine = Mesh(
        mesh.devices.reshape(n_half, n_row // n_x, n_x, n_col), ("half", "z", "x", "col")
    )
    row = ("z", "x")
    placed = (
        P(FRONT, "col"),
        P(FRONT, None, None),
        P(FRONT, None),
        P("half", row, None),
        P("half", "col", row),
        P("half", "col", row),
    )
    return jax.shard_map(
        shards,
        mesh=fine,
        in_specs=placed,
        out_specs=(P(FRONT, "col"), P(FRONT, "col")),
        check_vma=False,
    )
```

```python
import functools

import jax
import jax.numpy as jnp
from jax import lax
from jax.experimental import pallas as pl
from jax.experimental.pallas import tpu as pltpu
from jax.sharding import Mesh
from jax.sharding import PartitionSpec as P

BS = 64
NB = 8
HB = 8
LANES = 128
CHUNKS = 1
FRONT = ("half", "z", "x")
F32 = jnp.float32
BF16 = jnp.bfloat16
VMEM = pltpu.VMEM
SMEM = pltpu.SMEM


def whole(space):
    return pl.BlockSpec(memory_space=space)


def cost(flops, moved):
    return pl.CostEstimate(flops=flops, bytes_accessed=moved, transcendentals=0)


def grant(mib, **more):
    return pltpu.CompilerParams(vmem_limit_bytes=mib << 20, **more)


def swapped_halves(x):
    return pltpu.roll(x.astype(F32), BS, 1).astype(BF16)


def low_lanes(shape):
    return lax.broadcasted_iota(jnp.int32, shape, 1) < BS


def pack_kernel(map_ref, left_ref, right_ref, *out_refs):
    ranks = left_ref.shape[0] // len(out_refs)
    low = low_lanes((ranks, LANES))
    for k in range(left_ref.shape[1] // LANES):
        one, two = map_ref[2 * k], map_ref[2 * k + 1]
        for part, out_ref in enumerate(out_refs):
            rows = slice(part * ranks, (part + 1) * ranks)
            left = left_ref[rows, k * LANES : (k + 1) * LANES]
            right = right_ref[rows, k * LANES : (k + 1) * LANES]
            out_ref[one] = jnp.where(low, left, swapped_halves(right))
            out_ref[two] = jnp.where(low, swapped_halves(left), right)


def pack(order_map, left, right):
    ranks, width = left.shape
    out = jax.ShapeDtypeStruct((width // BS, ranks // CHUNKS, LANES), BF16)
    return pl.pallas_call(
        pack_kernel,
        out_shape=(out,) * CHUNKS,
        in_specs=[whole(SMEM), whole(VMEM), whole(VMEM)],
        out_specs=(whole(VMEM),) * CHUNKS,
        cost_estimate=cost(0, 8 * ranks * width),
        name="pack",
    )(order_map, left, right)


def sparse_kernel(
    cols_ref, a_ref, own_ref, low_ref, high_ref, range_ref, rows_ref, up_ref, down_ref, padded, spread
):
    per = a_ref.shape[0]
    count = own_ref.shape[0]
    step = pl.program_id(0)

    @pl.when(step == 0)
    def _():
        padded[:HB] = low_ref[...]
        padded[HB : HB + count] = own_ref[...]
        padded[HB + count :] = high_ref[...]
        spread[...] = jnp.zeros_like(spread)

    for i in range(per):
        b = step * per + i
        at = [cols_ref[b, t] for t in range(NB)]
        picked = jnp.concatenate([padded[c] for c in at], axis=0)
        a = a_ref[i]
        range_ref[i] = jnp.dot(a, picked, preferred_element_type=F32)
        terms = lax.dot_general(
            a, own_ref[b], (((0,), (0,)), ((), ())), preferred_element_type=F32
        )
        for t in range(NB):
            spread[at[t]] += terms[t * BS : (t + 1) * BS]

    @pl.when(step == pl.num_programs(0) - 1)
    def _():
        rows_ref[...] = spread[HB : HB + count]
        up_ref[...] = spread[HB + count :].astype(BF16)
        down_ref[...] = spread[:HB].astype(BF16)


def sparse(local_cols, couplings, blocks, low, high):
    count, _, width = blocks.shape
    per = 8
    edge = jax.ShapeDtypeStruct((HB, BS, width), BF16)
    return pl.pallas_call(
        sparse_kernel,
        grid=(count // per,),
        out_shape=(
            jax.ShapeDtypeStruct((count, BS, width), F32),
            jax.ShapeDtypeStruct((count, BS, width), F32),
            edge,
            edge,
        ),
        in_specs=[
            whole(SMEM),
            pl.BlockSpec((per, BS, NB * BS), lambda i: (i, 0, 0)),
            whole(VMEM),
            whole(VMEM),
            whole(VMEM),
        ],
        out_specs=(
            pl.BlockSpec((per, BS, width), lambda i: (i, 0, 0)),
            whole(VMEM),
            whole(VMEM),
            whole(VMEM),
        ),
        scratch_shapes=[
            pltpu.VMEM((count + 2 * HB, BS, width), BF16),
            pltpu.VMEM((count + 2 * HB, BS, width), F32),
        ],
        compiler_params=grant(12, dimension_semantics=("arbitrary",)),
        cost_estimate=cost(4 * count * BS * BS * NB * width, 6 << 20),
        name="sparse",
    )(local_cols, couplings, blocks, low, high)


def reduce_kernel(at_ref, gen_ref, own_ref, other_ref, out_ref, lhs):
    half, me = at_ref[0], at_ref[1]
    blocks, ranks, _ = gen_ref.shape
    count = blocks // 2
    parts = own_ref.shape[0]
    low = low_lanes((ranks, LANES))
    for side, first in ((0, half * count), (1, (1 - half) * count)):
        for k in range(count // 2):
            one, two = gen_ref[first + 2 * k], gen_ref[first + 2 * k + 1]
            lanes = slice(k * LANES, (k + 1) * LANES)
            lhs[side, :ranks, lanes] = jnp.where(low, one, swapped_halves(two))
            lhs[side, ranks:, lanes] = jnp.where(low, swapped_halves(one), two)
    for pair in range(0, parts, 2):
        total = 0.0
        for side, ref in ((0, own_ref), (1, other_ref)):
            rhs = jnp.concatenate([ref[pair], ref[pair + 1]], axis=1)
            total += jnp.dot(lhs[side], rhs, preferred_element_type=F32)
        for k in range(2):
            piece = total[:, k * LANES : (k + 1) * LANES]
            slot = lax.rem(me + parts - (pair + k), parts)
            out_ref[:, slot] = piece.reshape(out_ref.shape[0], -1, LANES).astype(BF16)


def reduced(at, gens, own, other, splits):
    _, ranks, _ = gens.shape
    parts, rows, _ = own.shape
    out = jax.ShapeDtypeStruct((splits, parts, 2 * ranks // splits, LANES), BF16)
    return pl.pallas_call(
        reduce_kernel,
        out_shape=out,
        in_specs=[whole(SMEM)] + [whole(VMEM)] * 3,
        out_specs=whole(VMEM),
        scratch_shapes=[pltpu.VMEM((2, 2 * ranks, rows), BF16)],
        compiler_params=grant(14),
        cost_estimate=cost(8 * ranks * rows * parts * LANES, 6 << 20),
        name="partials",
    )(at, gens, own, other)


def low_rank_kernel(mine, pieces, at_ref, *refs):
    gens, w_ref, refs = refs[:pieces], refs[pieces], refs[pieces + 1 :]
    me, step, steps = at_ref[1], pl.program_id(0), pl.num_programs(0)
    per, ranks, _ = gens[0].shape
    lhs = refs[-1]
    parts = lhs.shape[1] // ranks
    low = low_lanes((LANES, LANES))

    @pl.when(step == 0)
    def _():
        for k in range(parts):
            both = w_ref[:, lax.rem(me + parts - k, parts)].reshape(2 * ranks, LANES)
            turned = both.astype(F32).T.astype(BF16)
            lanes = slice(k * ranks, (k + 1) * ranks)
            lhs[:LANES, lanes] = turned[:, ranks:]
            lhs[LANES:, lanes] = turned[:, :ranks]

    for i in range(0, per, 2):
        rhs = jnp.concatenate(
            [jnp.concatenate([g[i + j] for g in gens], axis=0) for j in range(2)], axis=1
        )
        both = jnp.dot(lhs[...], rhs, preferred_element_type=F32)
        for j in range(2):
            lanes = slice(j * LANES, (j + 1) * LANES)
            out = jnp.where(low, both[:LANES, lanes], both[LANES:, lanes]).T
            for_range, for_rows = out[:BS], out[BS:]
            b = i + j
            if mine:
                sr_ref, sp_ref, below_ref, above_ref, range_ref, rows_ref = refs[:-1]
                range_ref[b] = for_range + sr_ref[b]
                for_rows += sp_ref[b]
                for_rows += jnp.where(step == 0, below_ref[b].astype(F32), 0.0)
                for_rows += jnp.where(step == steps - 1, above_ref[b].astype(F32), 0.0)
                rows_ref[b] = for_rows
            else:
                refs[0][0, b] = for_range.astype(BF16)
                refs[0][1, b] = for_rows.astype(BF16)


def low_rank(at, gens, w, added=()):
    blocks, _, _ = gens[0].shape
    count, per = blocks // 2, HB
    steps = count // per
    mine = bool(added)
    depth = sum(g.shape[1] for g in gens)

    def place(i, at_ref):
        half = at_ref[0] if mine else 1 - at_ref[0]
        return (half * steps + i, 0, 0)

    def tiles(rows):
        return pl.BlockSpec((per, rows, LANES), place)

    flat = pl.BlockSpec((per, BS, LANES), lambda i, at_ref: (i, 0, 0))
    edges = [flat] * 2 + [whole(VMEM)] * 2
    if mine:
        out_shape = (jax.ShapeDtypeStruct((count, BS, LANES), F32),) * 2
        out_specs = (flat, flat)
    else:
        out_shape = jax.ShapeDtypeStruct((2, count, BS, LANES), BF16)
        out_specs = pl.BlockSpec((2, per, BS, LANES), lambda i, at_ref: (0, i, 0, 0))
    return pl.pallas_call(
        functools.partial(low_rank_kernel, mine, len(gens)),
        grid_spec=pltpu.PrefetchScalarGridSpec(
            num_scalar_prefetch=1,
            grid=(steps,),
            in_specs=[tiles(g.shape[1]) for g in gens] + [whole(VMEM)] + (edges if mine else []),
            out_specs=out_specs,
            scratch_shapes=[pltpu.VMEM((2 * LANES, depth), BF16)],
        ),
        out_shape=out_shape,
        compiler_params=grant(10, dimension_semantics=("arbitrary",)),
        cost_estimate=cost(4 * count * LANES * depth * LANES, 4 << 20),
        name="mine" if mine else "theirs",
    )(at, *gens, w, *added)


def around(x, axis, by):
    count = lax.axis_size(axis)
    return lax.ppermute(x, axis, [(i, (i + by) % count) for i in range(count)])


def along_front(x, by):
    count = lax.axis_size(FRONT)
    pairs = [(i, i + by) for i in range(count) if 0 <= i + by < count]
    return lax.ppermute(x, FRONT, pairs)


def spread_out(x, axis):
    return lax.all_to_all(x, axis, split_axis=0, concat_axis=0, tiled=True)


def shards(samples, couplings, coupling_cols, child_map, gen_left, gen_right):
    count = couplings.shape[0]
    width = samples.shape[1]
    half, me = lax.axis_index("half"), lax.axis_index("col")
    at = jnp.stack([half, me]).astype(jnp.int32)
    n_z, n_x, n_col = (lax.axis_size(a) for a in ("z", "x", "col"))
    blocks = samples.reshape(count, BS, width)

    (packed,) = pack(child_map[0, 0], gen_left[0], gen_right[0])
    gens = spread_out(packed, ("z", "x"))

    shifted = [around(samples, "col", k) for k in range(1, n_col)]
    panels = jnp.stack([samples, *shifted])
    others = around(panels, "half", 1)
    low = along_front(blocks[count - HB :], 1)
    high = along_front(blocks[:HB], -1)

    local_cols = coupling_cols - lax.axis_index(FRONT) * count + HB
    gens, panels, others, local_cols = lax.optimization_barrier((gens, panels, others, local_cols))
    partial = reduced(at, gens, panels, others, n_z)

    middle = gens.shape[1] // 2
    first, second = gens[:, :middle], gens[:, middle:]
    up_a, down_b = around(first, "col", 1), around(second, "col", -1)
    up_b, down_a = around(second, "col", 1), around(first, "col", -1)
    far_a, far_b = around(up_a, "col", 1), around(down_b, "col", -1)
    sparse_range, sparse_rows, up, down = sparse(local_cols, couplings, blocks, low, high)
    by_z = spread_out(partial, "z")
    by_z, up, down = lax.optimization_barrier((by_z, up, down))
    below, above = along_front(up, 1), along_front(down, -1)
    at_last, below, above = lax.optimization_barrier((at, below, above))
    added = (sparse_range, sparse_rows, below, above)

    by_z = jnp.sum(by_z.astype(F32), axis=0)
    copies = jnp.broadcast_to(by_z, (n_x, *by_z.shape)).reshape(n_x * n_col, *by_z.shape[1:])
    arrived = spread_out(copies, ("x", "col"))
    slice_sum = jnp.sum(arrived.reshape(n_x, n_col, *by_z.shape[1:]), axis=0).astype(BF16)
    copies = jnp.broadcast_to(slice_sum, (n_z, *slice_sum.shape))
    w = spread_out(copies, "z")

    everyone = (gens, up_a, up_b, far_a, far_b, down_a, down_b)
    received = around(low_rank(at_last, everyone, w), "half", 1)
    range_out, rows_out = (
        (ours + theirs.astype(F32)).astype(BF16)
        for ours, theirs in zip(low_rank(at_last, everyone, w, added), received)
    )
    return range_out.reshape(samples.shape), rows_out.reshape(samples.shape)


def solution(mesh):
    n_half, n_row, n_col = (mesh.shape[a] for a in ("half", "row", "col"))
    n_x = n_col
    fine = Mesh(
        mesh.devices.reshape(n_half, n_row // n_x, n_x, n_col), ("half", "z", "x", "col")
    )
    row = ("z", "x")
    placed = (
        P(FRONT, "col"),
        P(FRONT, None, None),
        P(FRONT, None),
        P("half", row, None),
        P("half", "col", row),
        P("half", "col", row),
    )
    return jax.shard_map(
        shards,
        mesh=fine,
        in_specs=placed,
        out_specs=(P(FRONT, "col"), P(FRONT, "col")),
        check_vma=False,
    )
```

```python
import functools

import jax
import jax.numpy as jnp
from jax import lax
from jax.experimental import pallas as pl
from jax.experimental.pallas import tpu as pltpu
from jax.sharding import Mesh
from jax.sharding import PartitionSpec as P

BS = 64
NB = 8
HB = 8
LANES = 128
CHUNKS = 2
FRONT = ("half", "z", "x")
F32 = jnp.float32
BF16 = jnp.bfloat16
VMEM = pltpu.VMEM
SMEM = pltpu.SMEM


def whole(space):
    return pl.BlockSpec(memory_space=space)


def cost(flops, moved):
    return pl.CostEstimate(flops=flops, bytes_accessed=moved, transcendentals=0)


def grant(mib, **more):
    return pltpu.CompilerParams(vmem_limit_bytes=mib << 20, **more)


def swapped_halves(x):
    return pltpu.roll(x.astype(F32), BS, 1).astype(BF16)


def low_lanes(shape):
    return lax.broadcasted_iota(jnp.int32, shape, 1) < BS


def pack_kernel(map_ref, left_ref, right_ref, *out_refs):
    ranks = left_ref.shape[0] // len(out_refs)
    low = low_lanes((ranks, LANES))
    for k in range(left_ref.shape[1] // LANES):
        one, two = map_ref[2 * k], map_ref[2 * k + 1]
        for part, out_ref in enumerate(out_refs):
            rows = slice(part * ranks, (part + 1) * ranks)
            left = left_ref[rows, k * LANES : (k + 1) * LANES]
            right = right_ref[rows, k * LANES : (k + 1) * LANES]
            out_ref[one] = jnp.where(low, left, swapped_halves(right))
            out_ref[two] = jnp.where(low, swapped_halves(left), right)


def pack(order_map, left, right):
    ranks, width = left.shape
    out = jax.ShapeDtypeStruct((width // BS, ranks // CHUNKS, LANES), BF16)
    return pl.pallas_call(
        pack_kernel,
        out_shape=(out,) * CHUNKS,
        in_specs=[whole(SMEM), whole(VMEM), whole(VMEM)],
        out_specs=(whole(VMEM),) * CHUNKS,
        cost_estimate=cost(0, 8 * ranks * width),
        name="pack",
    )(order_map, left, right)


def sparse_kernel(
    cols_ref, a_ref, own_ref, low_ref, high_ref, range_ref, rows_ref, up_ref, down_ref, padded, spread
):
    per = a_ref.shape[0]
    count = own_ref.shape[0]
    step = pl.program_id(0)

    @pl.when(step == 0)
    def _():
        padded[:HB] = low_ref[...]
        padded[HB : HB + count] = own_ref[...]
        padded[HB + count :] = high_ref[...]
        spread[...] = jnp.zeros_like(spread)

    for i in range(per):
        b = step * per + i
        at = [cols_ref[b, t] for t in range(NB)]
        picked = jnp.concatenate([padded[c] for c in at], axis=0)
        a = a_ref[i]
        range_ref[i] = jnp.dot(a, picked, preferred_element_type=F32)
        terms = lax.dot_general(
            a, own_ref[b], (((0,), (0,)), ((), ())), preferred_element_type=F32
        )
        for t in range(NB):
            spread[at[t]] += terms[t * BS : (t + 1) * BS]

    @pl.when(step == pl.num_programs(0) - 1)
    def _():
        rows_ref[...] = spread[HB : HB + count]
        up_ref[...] = spread[HB + count :].astype(BF16)
        down_ref[...] = spread[:HB].astype(BF16)


def sparse(local_cols, couplings, blocks, low, high):
    count, _, width = blocks.shape
    per = 8
    edge = jax.ShapeDtypeStruct((HB, BS, width), BF16)
    return pl.pallas_call(
        sparse_kernel,
        grid=(count // per,),
        out_shape=(
            jax.ShapeDtypeStruct((count, BS, width), F32),
            jax.ShapeDtypeStruct((count, BS, width), F32),
            edge,
            edge,
        ),
        in_specs=[
            whole(SMEM),
            pl.BlockSpec((per, BS, NB * BS), lambda i: (i, 0, 0)),
            whole(VMEM),
            whole(VMEM),
            whole(VMEM),
        ],
        out_specs=(
            pl.BlockSpec((per, BS, width), lambda i: (i, 0, 0)),
            whole(VMEM),
            whole(VMEM),
            whole(VMEM),
        ),
        scratch_shapes=[
            pltpu.VMEM((count + 2 * HB, BS, width), BF16),
            pltpu.VMEM((count + 2 * HB, BS, width), F32),
        ],
        compiler_params=grant(12, dimension_semantics=("arbitrary",)),
        cost_estimate=cost(4 * count * BS * BS * NB * width, 6 << 20),
        name="sparse",
    )(local_cols, couplings, blocks, low, high)


def reduce_kernel(at_ref, *refs):
    gen_refs, (own_ref, other_ref, out_ref, lhs) = refs[:CHUNKS], refs[CHUNKS:]
    half, me = at_ref[0], at_ref[1]
    blocks, ranks, _ = gen_refs[0].shape
    count = blocks // 2
    parts = own_ref.shape[0]
    low = low_lanes((ranks, LANES))
    for side, first in ((0, half * count), (1, (1 - half) * count)):
        for part, gen_ref in enumerate(gen_refs):
            left = slice(part * ranks, (part + 1) * ranks)
            right = slice((CHUNKS + part) * ranks, (CHUNKS + part + 1) * ranks)
            for k in range(count // 2):
                one, two = gen_ref[first + 2 * k], gen_ref[first + 2 * k + 1]
                lanes = slice(k * LANES, (k + 1) * LANES)
                lhs[side, left, lanes] = jnp.where(low, one, swapped_halves(two))
                lhs[side, right, lanes] = jnp.where(low, swapped_halves(one), two)
    for pair in range(0, parts, 2):
        total = 0.0
        for side, ref in ((0, own_ref), (1, other_ref)):
            rhs = jnp.concatenate([ref[pair], ref[pair + 1]], axis=1)
            total += jnp.dot(lhs[side], rhs, preferred_element_type=F32)
        for k in range(2):
            piece = total[:, k * LANES : (k + 1) * LANES]
            slot = lax.rem(me + parts - (pair + k), parts)
            out_ref[:, slot] = piece.reshape(out_ref.shape[0], -1, LANES).astype(BF16)


def reduced(at, gens, own, other, splits):
    ranks = CHUNKS * gens[0].shape[1]
    parts, rows, _ = own.shape
    out = jax.ShapeDtypeStruct((splits, parts, 2 * ranks // splits, LANES), BF16)
    return pl.pallas_call(
        reduce_kernel,
        out_shape=out,
        in_specs=[whole(SMEM)] + [whole(VMEM)] * (CHUNKS + 2),
        out_specs=whole(VMEM),
        scratch_shapes=[pltpu.VMEM((2, 2 * ranks, rows), BF16)],
        compiler_params=grant(14),
        cost_estimate=cost(8 * ranks * rows * parts * LANES, 6 << 20),
        name="partials",
    )(at, *gens, own, other)


def low_rank_kernel(mine, pieces, at_ref, *refs):
    gens, w_ref, refs = refs[:pieces], refs[pieces], refs[pieces + 1 :]
    me, step, steps = at_ref[1], pl.program_id(0), pl.num_programs(0)
    per = gens[0].shape[0]
    lhs = refs[-1]
    parts = w_ref.shape[1]
    ranks = lhs.shape[1] // parts
    low = low_lanes((LANES, LANES))

    @pl.when(step == 0)
    def _():
        for k in range(parts):
            both = w_ref[:, lax.rem(me + parts - k, parts)].reshape(2 * ranks, LANES)
            turned = both.astype(F32).T.astype(BF16)
            lanes = slice(k * ranks, (k + 1) * ranks)
            lhs[:LANES, lanes] = turned[:, ranks:]
            lhs[LANES:, lanes] = turned[:, :ranks]

    for i in range(0, per, 2):
        rhs = jnp.concatenate(
            [jnp.concatenate([g[i + j] for g in gens], axis=0) for j in range(2)], axis=1
        )
        both = jnp.dot(lhs[...], rhs, preferred_element_type=F32)
        for j in range(2):
            lanes = slice(j * LANES, (j + 1) * LANES)
            out = jnp.where(low, both[:LANES, lanes], both[LANES:, lanes]).T
            for_range, for_rows = out[:BS], out[BS:]
            b = i + j
            if mine:
                sr_ref, sp_ref, below_ref, above_ref, range_ref, rows_ref = refs[:-1]
                range_ref[b] = for_range + sr_ref[b]
                for_rows += sp_ref[b]
                for_rows += jnp.where(step == 0, below_ref[b].astype(F32), 0.0)
                for_rows += jnp.where(step == steps - 1, above_ref[b].astype(F32), 0.0)
                rows_ref[b] = for_rows
            else:
                refs[0][0, b] = for_range.astype(BF16)
                refs[0][1, b] = for_rows.astype(BF16)


def low_rank(at, gens, w, added=()):
    blocks = gens[0].shape[0]
    count, per = blocks // 2, HB
    steps = count // per
    mine = bool(added)
    depth = sum(g.shape[1] for g in gens)

    def place(i, at_ref):
        half = at_ref[0] if mine else 1 - at_ref[0]
        return (half * steps + i, 0, 0)

    def tiles(rows):
        return pl.BlockSpec((per, rows, LANES), place)

    flat = pl.BlockSpec((per, BS, LANES), lambda i, at_ref: (i, 0, 0))
    edges = [flat] * 2 + [whole(VMEM)] * 2
    if mine:
        out_shape = (jax.ShapeDtypeStruct((count, BS, LANES), F32),) * 2
        out_specs = (flat, flat)
    else:
        out_shape = jax.ShapeDtypeStruct((2, count, BS, LANES), BF16)
        out_specs = pl.BlockSpec((2, per, BS, LANES), lambda i, at_ref: (0, i, 0, 0))
    return pl.pallas_call(
        functools.partial(low_rank_kernel, mine, len(gens)),
        grid_spec=pltpu.PrefetchScalarGridSpec(
            num_scalar_prefetch=1,
            grid=(steps,),
            in_specs=[tiles(g.shape[1]) for g in gens] + [whole(VMEM)] + (edges if mine else []),
            out_specs=out_specs,
            scratch_shapes=[pltpu.VMEM((2 * LANES, depth), BF16)],
        ),
        out_shape=out_shape,
        compiler_params=grant(10, dimension_semantics=("arbitrary",)),
        cost_estimate=cost(4 * count * LANES * depth * LANES, 4 << 20),
        name="mine" if mine else "theirs",
    )(at, *gens, w, *added)


def around(x, axis, by):
    count = lax.axis_size(axis)
    return lax.ppermute(x, axis, [(i, (i + by) % count) for i in range(count)])


def along_front(x, by):
    count = lax.axis_size(FRONT)
    pairs = [(i, i + by) for i in range(count) if 0 <= i + by < count]
    return lax.ppermute(x, FRONT, pairs)


def spread_out(x, axis):
    return lax.all_to_all(x, axis, split_axis=0, concat_axis=0, tiled=True)


def shards(samples, couplings, coupling_cols, child_map, gen_left, gen_right):
    count = couplings.shape[0]
    width = samples.shape[1]
    half, me = lax.axis_index("half"), lax.axis_index("col")
    at = jnp.stack([half, me]).astype(jnp.int32)
    n_z, n_x, n_col = (lax.axis_size(a) for a in ("z", "x", "col"))
    blocks = samples.reshape(count, BS, width)

    packed_a, packed_b = pack(child_map[0, 0], gen_left[0], gen_right[0])
    gens_a = spread_out(packed_a, ("z", "x"))
    gens_b = spread_out(packed_b, ("z", "x"))

    shifted = [around(samples, "col", k) for k in range(1, n_col)]
    low = along_front(blocks[count - HB :], 1)
    high = along_front(blocks[:HB], -1)
    local_cols = coupling_cols - lax.axis_index(FRONT) * count + HB

    up_a, down_a = around(gens_a, "col", 1), around(gens_a, "col", -1)
    shifted, _ = lax.optimization_barrier((shifted, gens_a))
    panels = jnp.stack([samples, *shifted])
    others = around(panels, "half", 1)
    far_a = around(up_a, "col", 1)
    sparse_range, sparse_rows, up, down = sparse(local_cols, couplings, blocks, low, high)
    below, above = along_front(up, 1), along_front(down, -1)
    added = (sparse_range, sparse_rows, below, above)

    gens_b, panels, others, up, down = lax.optimization_barrier((gens_b, panels, others, up, down))
    partial = reduced(at, (gens_a, gens_b), panels, others, n_z)
    up_b, down_b = around(gens_b, "col", 1), around(gens_b, "col", -1)
    far_b = around(down_b, "col", -1)

    by_z = spread_out(partial, "z")
    by_z = jnp.sum(by_z.astype(F32), axis=0)
    copies = jnp.broadcast_to(by_z, (n_x, *by_z.shape)).reshape(n_x * n_col, *by_z.shape[1:])
    arrived = spread_out(copies, ("x", "col"))
    slice_sum = jnp.sum(arrived.reshape(n_x, n_col, *by_z.shape[1:]), axis=0).astype(BF16)
    copies = jnp.broadcast_to(slice_sum, (n_z, *slice_sum.shape))
    w = spread_out(copies, "z")

    everyone = (gens_a, gens_b, up_a, up_b, far_a, far_b, down_a, down_b)
    received = around(low_rank(at, everyone, w), "half", 1)
    range_out, rows_out = (
        (ours + theirs.astype(F32)).astype(BF16)
        for ours, theirs in zip(low_rank(at, everyone, w, added), received)
    )
    return range_out.reshape(samples.shape), rows_out.reshape(samples.shape)


def solution(mesh):
    n_half, n_row, n_col = (mesh.shape[a] for a in ("half", "row", "col"))
    n_x = n_col
    fine = Mesh(
        mesh.devices.reshape(n_half, n_row // n_x, n_x, n_col), ("half", "z", "x", "col")
    )
    row = ("z", "x")
    placed = (
        P(FRONT, "col"),
        P(FRONT, None, None),
        P(FRONT, None),
        P("half", row, None),
        P("half", "col", row),
        P("half", "col", row),
    )
    return jax.shard_map(
        shards,
        mesh=fine,
        in_specs=placed,
        out_specs=(P(FRONT, "col"), P(FRONT, "col")),
        check_vma=False,
    )
```

```python
import functools

import jax
import jax.numpy as jnp
from jax import lax
from jax.experimental import pallas as pl
from jax.experimental.pallas import tpu as pltpu
from jax.sharding import Mesh
from jax.sharding import PartitionSpec as P

BS = 64
NB = 8
HB = 8
LANES = 128
CHUNKS = 1
FRONT = ("half", "z", "x")
F32 = jnp.float32
BF16 = jnp.bfloat16
VMEM = pltpu.VMEM
SMEM = pltpu.SMEM


def whole(space):
    return pl.BlockSpec(memory_space=space)


def cost(flops, moved):
    return pl.CostEstimate(flops=flops, bytes_accessed=moved, transcendentals=0)


def grant(mib, **more):
    return pltpu.CompilerParams(vmem_limit_bytes=mib << 20, **more)


def swapped_halves(x):
    return pltpu.roll(x.astype(F32), BS, 1).astype(BF16)


def low_lanes(shape):
    return lax.broadcasted_iota(jnp.int32, shape, 1) < BS


def pack_kernel(map_ref, left_ref, right_ref, *out_refs):
    ranks = left_ref.shape[0] // len(out_refs)
    low = low_lanes((ranks, LANES))
    for k in range(left_ref.shape[1] // LANES):
        one, two = map_ref[2 * k], map_ref[2 * k + 1]
        for part, out_ref in enumerate(out_refs):
            rows = slice(part * ranks, (part + 1) * ranks)
            left = left_ref[rows, k * LANES : (k + 1) * LANES]
            right = right_ref[rows, k * LANES : (k + 1) * LANES]
            out_ref[one] = jnp.where(low, left, swapped_halves(right))
            out_ref[two] = jnp.where(low, swapped_halves(left), right)


def pack(order_map, left, right):
    ranks, width = left.shape
    out = jax.ShapeDtypeStruct((width // BS, ranks // CHUNKS, LANES), BF16)
    return pl.pallas_call(
        pack_kernel,
        out_shape=(out,) * CHUNKS,
        in_specs=[whole(SMEM), whole(VMEM), whole(VMEM)],
        out_specs=(whole(VMEM),) * CHUNKS,
        cost_estimate=cost(0, 8 * ranks * width),
        name="pack",
    )(order_map, left, right)


def sparse_kernel(
    cols_ref, a_ref, own_ref, low_ref, high_ref, range_ref, rows_ref, up_ref, down_ref, padded, spread
):
    per = a_ref.shape[0]
    count = own_ref.shape[0]
    step = pl.program_id(0)

    @pl.when(step == 0)
    def _():
        padded[:HB] = low_ref[...]
        padded[HB : HB + count] = own_ref[...]
        padded[HB + count :] = high_ref[...]
        spread[...] = jnp.zeros_like(spread)

    for i in range(per):
        b = step * per + i
        at = [cols_ref[b, t] for t in range(NB)]
        picked = jnp.concatenate([padded[c] for c in at], axis=0)
        a = a_ref[i]
        range_ref[i] = jnp.dot(a, picked, preferred_element_type=F32)
        terms = lax.dot_general(
            a, own_ref[b], (((0,), (0,)), ((), ())), preferred_element_type=F32
        )
        for t in range(NB):
            spread[at[t]] += terms[t * BS : (t + 1) * BS]

    @pl.when(step == pl.num_programs(0) - 1)
    def _():
        rows_ref[...] = spread[HB : HB + count]
        up_ref[...] = spread[HB + count :].astype(BF16)
        down_ref[...] = spread[:HB].astype(BF16)


def sparse(local_cols, couplings, blocks, low, high):
    count, _, width = blocks.shape
    per = 8
    edge = jax.ShapeDtypeStruct((HB, BS, width), BF16)
    return pl.pallas_call(
        sparse_kernel,
        grid=(count // per,),
        out_shape=(
            jax.ShapeDtypeStruct((count, BS, width), F32),
            jax.ShapeDtypeStruct((count, BS, width), F32),
            edge,
            edge,
        ),
        in_specs=[
            whole(SMEM),
            pl.BlockSpec((per, BS, NB * BS), lambda i: (i, 0, 0)),
            whole(VMEM),
            whole(VMEM),
            whole(VMEM),
        ],
        out_specs=(
            pl.BlockSpec((per, BS, width), lambda i: (i, 0, 0)),
            whole(VMEM),
            whole(VMEM),
            whole(VMEM),
        ),
        scratch_shapes=[
            pltpu.VMEM((count + 2 * HB, BS, width), BF16),
            pltpu.VMEM((count + 2 * HB, BS, width), F32),
        ],
        compiler_params=grant(12, dimension_semantics=("arbitrary",)),
        cost_estimate=cost(4 * count * BS * BS * NB * width, 6 << 20),
        name="sparse",
    )(local_cols, couplings, blocks, low, high)


def reduce_kernel(at_ref, gen_ref, own_ref, other_ref, out_ref, lhs):
    half, me = at_ref[0], at_ref[1]
    blocks, ranks, _ = gen_ref.shape
    count = blocks // 2
    parts = own_ref.shape[0]
    low = low_lanes((ranks, LANES))
    for side, first in ((0, half * count), (1, (1 - half) * count)):
        for k in range(count // 2):
            one, two = gen_ref[first + 2 * k], gen_ref[first + 2 * k + 1]
            lanes = slice(k * LANES, (k + 1) * LANES)
            lhs[side, :ranks, lanes] = jnp.where(low, one, swapped_halves(two))
            lhs[side, ranks:, lanes] = jnp.where(low, swapped_halves(one), two)
    for pair in range(0, parts, 2):
        total = 0.0
        for side, ref in ((0, own_ref), (1, other_ref)):
            rhs = jnp.concatenate([ref[pair], ref[pair + 1]], axis=1)
            total += jnp.dot(lhs[side], rhs, preferred_element_type=F32)
        for k in range(2):
            piece = total[:, k * LANES : (k + 1) * LANES]
            slot = lax.rem(me + parts - (pair + k), parts)
            out_ref[:, slot] = piece.reshape(out_ref.shape[0], -1, LANES).astype(BF16)


def reduced(at, gens, own, other, splits):
    _, ranks, _ = gens.shape
    parts, rows, _ = own.shape
    out = jax.ShapeDtypeStruct((splits, parts, 2 * ranks // splits, LANES), BF16)
    return pl.pallas_call(
        reduce_kernel,
        out_shape=out,
        in_specs=[whole(SMEM)] + [whole(VMEM)] * 3,
        out_specs=whole(VMEM),
        scratch_shapes=[pltpu.VMEM((2, 2 * ranks, rows), BF16)],
        compiler_params=grant(14),
        cost_estimate=cost(8 * ranks * rows * parts * LANES, 6 << 20),
        name="partials",
    )(at, gens, own, other)


def low_rank_kernel(mine, pieces, at_ref, *refs):
    gens, w_ref, refs = refs[:pieces], refs[pieces], refs[pieces + 1 :]
    me, step, steps = at_ref[1], pl.program_id(0), pl.num_programs(0)
    per, ranks, _ = gens[0].shape
    lhs = refs[-1]
    parts = lhs.shape[1] // ranks
    low = low_lanes((LANES, LANES))

    @pl.when(step == 0)
    def _():
        for k in range(parts):
            both = w_ref[:, lax.rem(me + parts - k, parts)].reshape(2 * ranks, LANES)
            turned = both.astype(F32).T.astype(BF16)
            lanes = slice(k * ranks, (k + 1) * ranks)
            lhs[:LANES, lanes] = turned[:, ranks:]
            lhs[LANES:, lanes] = turned[:, :ranks]

    for i in range(0, per, 2):
        rhs = jnp.concatenate(
            [jnp.concatenate([g[i + j] for g in gens], axis=0) for j in range(2)], axis=1
        )
        both = jnp.dot(lhs[...], rhs, preferred_element_type=F32)
        for j in range(2):
            lanes = slice(j * LANES, (j + 1) * LANES)
            out = jnp.where(low, both[:LANES, lanes], both[LANES:, lanes]).T
            for_range, for_rows = out[:BS], out[BS:]
            b = i + j
            if mine:
                sr_ref, sp_ref, below_ref, above_ref, range_ref, rows_ref = refs[:-1]
                range_ref[b] = for_range + sr_ref[b]
                for_rows += sp_ref[b]
                for_rows += jnp.where(step == 0, below_ref[b].astype(F32), 0.0)
                for_rows += jnp.where(step == steps - 1, above_ref[b].astype(F32), 0.0)
                rows_ref[b] = for_rows
            else:
                refs[0][0, b] = for_range.astype(BF16)
                refs[0][1, b] = for_rows.astype(BF16)


def low_rank(at, gens, w, added=()):
    blocks, _, _ = gens[0].shape
    count, per = blocks // 2, HB
    steps = count // per
    mine = bool(added)
    depth = sum(g.shape[1] for g in gens)

    def place(i, at_ref):
        half = at_ref[0] if mine else 1 - at_ref[0]
        return (half * steps + i, 0, 0)

    def tiles(rows):
        return pl.BlockSpec((per, rows, LANES), place)

    flat = pl.BlockSpec((per, BS, LANES), lambda i, at_ref: (i, 0, 0))
    edges = [flat] * 2 + [whole(VMEM)] * 2
    if mine:
        out_shape = (jax.ShapeDtypeStruct((count, BS, LANES), F32),) * 2
        out_specs = (flat, flat)
    else:
        out_shape = jax.ShapeDtypeStruct((2, count, BS, LANES), BF16)
        out_specs = pl.BlockSpec((2, per, BS, LANES), lambda i, at_ref: (0, i, 0, 0))
    return pl.pallas_call(
        functools.partial(low_rank_kernel, mine, len(gens)),
        grid_spec=pltpu.PrefetchScalarGridSpec(
            num_scalar_prefetch=1,
            grid=(steps,),
            in_specs=[tiles(g.shape[1]) for g in gens] + [whole(VMEM)] + (edges if mine else []),
            out_specs=out_specs,
            scratch_shapes=[pltpu.VMEM((2 * LANES, depth), BF16)],
        ),
        out_shape=out_shape,
        compiler_params=grant(10, dimension_semantics=("arbitrary",)),
        cost_estimate=cost(4 * count * LANES * depth * LANES, 4 << 20),
        name="mine" if mine else "theirs",
    )(at, *gens, w, *added)


def around(x, axis, by):
    count = lax.axis_size(axis)
    return lax.ppermute(x, axis, [(i, (i + by) % count) for i in range(count)])


def along_front(x, by):
    count = lax.axis_size(FRONT)
    pairs = [(i, i + by) for i in range(count) if 0 <= i + by < count]
    return lax.ppermute(x, FRONT, pairs)


def spread_out(x, axis):
    return lax.all_to_all(x, axis, split_axis=0, concat_axis=0, tiled=True)


def shards(samples, couplings, coupling_cols, child_map, gen_left, gen_right):
    count = couplings.shape[0]
    width = samples.shape[1]
    half, me = lax.axis_index("half"), lax.axis_index("col")
    at = jnp.stack([half, me]).astype(jnp.int32)
    n_z, n_x, n_col = (lax.axis_size(a) for a in ("z", "x", "col"))
    blocks = samples.reshape(count, BS, width)

    (packed,) = pack(child_map[0, 0], gen_left[0], gen_right[0])
    gens = spread_out(packed, ("z", "x"))

    shifted = [around(samples, "col", k) for k in range(1, n_col)]
    panels = jnp.stack([samples, *shifted])
    others = around(panels, "half", 1)
    low = along_front(blocks[count - HB :], 1)
    high = along_front(blocks[:HB], -1)

    local_cols = coupling_cols - lax.axis_index(FRONT) * count + HB
    gens, panels, others, local_cols = lax.optimization_barrier((gens, panels, others, local_cols))
    partial = reduced(at, gens, panels, others, n_z)

    middle = gens.shape[1] // 2
    first, second = gens[:, :middle], gens[:, middle:]
    up_a, down_b = around(first, "col", 1), around(second, "col", -1)
    up_b = around(second, "col", 1)
    down_a = around(first, "col", -1)
    far_a, far_b = around(up_a, "col", 1), around(down_b, "col", -1)
    sparse_range, sparse_rows, up, down = sparse(local_cols, couplings, blocks, low, high)
    by_z = spread_out(partial, "z")
    at_last, up, down = lax.optimization_barrier((at, up, down))
    below, above = along_front(up, 1), along_front(down, -1)
    added = (sparse_range, sparse_rows, below, above)

    by_z = jnp.sum(by_z.astype(F32), axis=0)
    copies = jnp.broadcast_to(by_z, (n_x, *by_z.shape)).reshape(n_x * n_col, *by_z.shape[1:])
    arrived = spread_out(copies, ("x", "col"))
    slice_sum = jnp.sum(arrived.reshape(n_x, n_col, *by_z.shape[1:]), axis=0).astype(BF16)
    copies = jnp.broadcast_to(slice_sum, (n_z, *slice_sum.shape))
    w = spread_out(copies, "z")

    everyone = (gens, up_a, up_b, far_a, far_b, down_a, down_b)
    theirs = low_rank(at_last, everyone, w)
    received = around(theirs, "half", 1)
    range_out, rows_out = (
        (mine + given.astype(F32)).astype(BF16)
        for mine, given in zip(low_rank(at_last, everyone, w, added), received)
    )
    return range_out.reshape(samples.shape), rows_out.reshape(samples.shape)


def solution(mesh):
    n_half, n_row, n_col = (mesh.shape[a] for a in ("half", "row", "col"))
    n_x = n_col
    fine = Mesh(
        mesh.devices.reshape(n_half, n_row // n_x, n_x, n_col), ("half", "z", "x", "col")
    )
    row = ("z", "x")
    placed = (
        P(FRONT, "col"),
        P(FRONT, None, None),
        P(FRONT, None),
        P("half", row, None),
        P("half", "col", row),
        P("half", "col", row),
    )
    return jax.shard_map(
        shards,
        mesh=fine,
        in_specs=placed,
        out_specs=(P(FRONT, "col"), P(FRONT, "col")),
        check_vma=False,
    )
```

```python
import functools

import jax
import jax.numpy as jnp
from jax import lax
from jax.experimental import pallas as pl
from jax.experimental.pallas import tpu as pltpu
from jax.sharding import Mesh
from jax.sharding import PartitionSpec as P

BS = 64
NB = 8
HB = 8
LANES = 128
CHUNKS = 1
FRONT = ("half", "z", "x")
F32 = jnp.float32
BF16 = jnp.bfloat16
VMEM = pltpu.VMEM
SMEM = pltpu.SMEM


def whole(space):
    return pl.BlockSpec(memory_space=space)


def cost(flops, moved):
    return pl.CostEstimate(flops=flops, bytes_accessed=moved, transcendentals=0)


def grant(mib, **more):
    return pltpu.CompilerParams(vmem_limit_bytes=mib << 20, **more)


def swapped_halves(x):
    return pltpu.roll(x.astype(F32), BS, 1).astype(BF16)


def low_lanes(shape):
    return lax.broadcasted_iota(jnp.int32, shape, 1) < BS


def pack_kernel(map_ref, left_ref, right_ref, own_ref, head_ref, tail_ref, *out_refs):
    head_ref[...] = own_ref[:HB]
    tail_ref[...] = own_ref[own_ref.shape[0] - HB :]
    ranks = left_ref.shape[0] // len(out_refs)
    low = low_lanes((ranks, LANES))
    for k in range(left_ref.shape[1] // LANES):
        one, two = map_ref[2 * k], map_ref[2 * k + 1]
        for part, out_ref in enumerate(out_refs):
            rows = slice(part * ranks, (part + 1) * ranks)
            left = left_ref[rows, k * LANES : (k + 1) * LANES]
            right = right_ref[rows, k * LANES : (k + 1) * LANES]
            out_ref[one] = jnp.where(low, left, swapped_halves(right))
            out_ref[two] = jnp.where(low, swapped_halves(left), right)


def pack(order_map, left, right, blocks):
    ranks, width = left.shape
    out = jax.ShapeDtypeStruct((width // BS, ranks // CHUNKS, LANES), BF16)
    edge = jax.ShapeDtypeStruct((HB, *blocks.shape[1:]), BF16)
    return pl.pallas_call(
        pack_kernel,
        out_shape=(edge, edge, *(out,) * CHUNKS),
        in_specs=[whole(SMEM)] + [whole(VMEM)] * 3,
        out_specs=(whole(VMEM),) * (2 + CHUNKS),
        cost_estimate=cost(0, 8 * ranks * width),
        name="pack",
    )(order_map, left, right, blocks)


def sparse_kernel(
    cols_ref, a_ref, own_ref, low_ref, high_ref, range_ref, rows_ref, up_ref, down_ref, padded, spread
):
    per = a_ref.shape[0]
    count = own_ref.shape[0]
    step = pl.program_id(0)

    @pl.when(step == 0)
    def _():
        padded[:HB] = low_ref[...]
        padded[HB : HB + count] = own_ref[...]
        padded[HB + count :] = high_ref[...]
        spread[...] = jnp.zeros_like(spread)

    for i in range(per):
        b = step * per + i
        at = [cols_ref[b, t] for t in range(NB)]
        picked = jnp.concatenate([padded[c] for c in at], axis=0)
        a = a_ref[i]
        range_ref[i] = jnp.dot(a, picked, preferred_element_type=F32)
        terms = lax.dot_general(
            a, own_ref[b], (((0,), (0,)), ((), ())), preferred_element_type=F32
        )
        for t in range(NB):
            spread[at[t]] += terms[t * BS : (t + 1) * BS]

    @pl.when(step == pl.num_programs(0) - 1)
    def _():
        rows_ref[...] = spread[HB : HB + count]
        up_ref[...] = spread[HB + count :].astype(BF16)
        down_ref[...] = spread[:HB].astype(BF16)


def sparse(local_cols, couplings, blocks, low, high):
    count, _, width = blocks.shape
    per = 8
    edge = jax.ShapeDtypeStruct((HB, BS, width), BF16)
    return pl.pallas_call(
        sparse_kernel,
        grid=(count // per,),
        out_shape=(
            jax.ShapeDtypeStruct((count, BS, width), F32),
            jax.ShapeDtypeStruct((count, BS, width), F32),
            edge,
            edge,
        ),
        in_specs=[
            whole(SMEM),
            pl.BlockSpec((per, BS, NB * BS), lambda i: (i, 0, 0)),
            whole(VMEM),
            whole(VMEM),
            whole(VMEM),
        ],
        out_specs=(
            pl.BlockSpec((per, BS, width), lambda i: (i, 0, 0)),
            whole(VMEM),
            whole(VMEM),
            whole(VMEM),
        ),
        scratch_shapes=[
            pltpu.VMEM((count + 2 * HB, BS, width), BF16),
            pltpu.VMEM((count + 2 * HB, BS, width), F32),
        ],
        compiler_params=grant(12, dimension_semantics=("arbitrary",)),
        cost_estimate=cost(4 * count * BS * BS * NB * width, 6 << 20),
        name="sparse",
    )(local_cols, couplings, blocks, low, high)


def reduce_kernel(at_ref, gen_ref, own_ref, other_ref, out_ref, lhs):
    half, me = at_ref[0], at_ref[1]
    blocks, ranks, _ = gen_ref.shape
    count = blocks // 2
    parts = own_ref.shape[0]
    low = low_lanes((ranks, LANES))
    for side, first in ((0, half * count), (1, (1 - half) * count)):
        for k in range(count // 2):
            one, two = gen_ref[first + 2 * k], gen_ref[first + 2 * k + 1]
            lanes = slice(k * LANES, (k + 1) * LANES)
            lhs[side, :ranks, lanes] = jnp.where(low, one, swapped_halves(two))
            lhs[side, ranks:, lanes] = jnp.where(low, swapped_halves(one), two)
    for pair in range(0, parts, 2):
        total = 0.0
        for side, ref in ((0, own_ref), (1, other_ref)):
            rhs = jnp.concatenate([ref[pair], ref[pair + 1]], axis=1)
            total += jnp.dot(lhs[side], rhs, preferred_element_type=F32)
        for k in range(2):
            piece = total[:, k * LANES : (k + 1) * LANES]
            slot = lax.rem(me + parts - (pair + k), parts)
            out_ref[:, slot] = piece.reshape(out_ref.shape[0], -1, LANES).astype(BF16)


def reduced(at, gens, own, other, splits):
    _, ranks, _ = gens.shape
    parts, rows, _ = own.shape
    out = jax.ShapeDtypeStruct((splits, parts, 2 * ranks // splits, LANES), BF16)
    return pl.pallas_call(
        reduce_kernel,
        out_shape=out,
        in_specs=[whole(SMEM)] + [whole(VMEM)] * 3,
        out_specs=whole(VMEM),
        scratch_shapes=[pltpu.VMEM((2, 2 * ranks, rows), BF16)],
        compiler_params=grant(14),
        cost_estimate=cost(8 * ranks * rows * parts * LANES, 6 << 20),
        name="partials",
    )(at, gens, own, other)


def low_rank_kernel(mine, pieces, at_ref, *refs):
    gens, w_ref, refs = refs[:pieces], refs[pieces], refs[pieces + 1 :]
    me, step, steps = at_ref[1], pl.program_id(0), pl.num_programs(0)
    per, ranks, _ = gens[0].shape
    lhs = refs[-1]
    parts = lhs.shape[1] // ranks
    low = low_lanes((LANES, LANES))

    @pl.when(step == 0)
    def _():
        for k in range(parts):
            both = w_ref[:, lax.rem(me + parts - k, parts)].reshape(2 * ranks, LANES)
            turned = both.astype(F32).T.astype(BF16)
            lanes = slice(k * ranks, (k + 1) * ranks)
            lhs[:LANES, lanes] = turned[:, ranks:]
            lhs[LANES:, lanes] = turned[:, :ranks]

    for i in range(0, per, 2):
        rhs = jnp.concatenate(
            [jnp.concatenate([g[i + j] for g in gens], axis=0) for j in range(2)], axis=1
        )
        both = jnp.dot(lhs[...], rhs, preferred_element_type=F32)
        for j in range(2):
            lanes = slice(j * LANES, (j + 1) * LANES)
            out = jnp.where(low, both[:LANES, lanes], both[LANES:, lanes]).T
            for_range, for_rows = out[:BS], out[BS:]
            b = i + j
            if mine:
                sr_ref, sp_ref, below_ref, above_ref, range_ref, rows_ref = refs[:-1]
                range_ref[b] = for_range + sr_ref[b]
                for_rows += sp_ref[b]
                for_rows += jnp.where(step == 0, below_ref[b].astype(F32), 0.0)
                for_rows += jnp.where(step == steps - 1, above_ref[b].astype(F32), 0.0)
                rows_ref[b] = for_rows
            else:
                refs[0][0, b] = for_range.astype(BF16)
                refs[0][1, b] = for_rows.astype(BF16)


def low_rank(at, gens, w, added=()):
    blocks, _, _ = gens[0].shape
    count, per = blocks // 2, HB
    steps = count // per
    mine = bool(added)
    depth = sum(g.shape[1] for g in gens)

    def place(i, at_ref):
        half = at_ref[0] if mine else 1 - at_ref[0]
        return (half * steps + i, 0, 0)

    def tiles(rows):
        return pl.BlockSpec((per, rows, LANES), place)

    flat = pl.BlockSpec((per, BS, LANES), lambda i, at_ref: (i, 0, 0))
    edges = [flat] * 2 + [whole(VMEM)] * 2
    if mine:
        out_shape = (jax.ShapeDtypeStruct((count, BS, LANES), F32),) * 2
        out_specs = (flat, flat)
    else:
        out_shape = jax.ShapeDtypeStruct((2, count, BS, LANES), BF16)
        out_specs = pl.BlockSpec((2, per, BS, LANES), lambda i, at_ref: (0, i, 0, 0))
    return pl.pallas_call(
        functools.partial(low_rank_kernel, mine, len(gens)),
        grid_spec=pltpu.PrefetchScalarGridSpec(
            num_scalar_prefetch=1,
            grid=(steps,),
            in_specs=[tiles(g.shape[1]) for g in gens] + [whole(VMEM)] + (edges if mine else []),
            out_specs=out_specs,
            scratch_shapes=[pltpu.VMEM((2 * LANES, depth), BF16)],
        ),
        out_shape=out_shape,
        compiler_params=grant(10, dimension_semantics=("arbitrary",)),
        cost_estimate=cost(4 * count * LANES * depth * LANES, 4 << 20),
        name="mine" if mine else "theirs",
    )(at, *gens, w, *added)


def around(x, axis, by):
    count = lax.axis_size(axis)
    return lax.ppermute(x, axis, [(i, (i + by) % count) for i in range(count)])


def along_front(x, by):
    count = lax.axis_size(FRONT)
    pairs = [(i, i + by) for i in range(count) if 0 <= i + by < count]
    return lax.ppermute(x, FRONT, pairs)


def spread_out(x, axis):
    return lax.all_to_all(x, axis, split_axis=0, concat_axis=0, tiled=True)


def shards(samples, couplings, coupling_cols, child_map, gen_left, gen_right):
    count = couplings.shape[0]
    width = samples.shape[1]
    half, me = lax.axis_index("half"), lax.axis_index("col")
    at = jnp.stack([half, me]).astype(jnp.int32)
    n_z, n_x, n_col = (lax.axis_size(a) for a in ("z", "x", "col"))
    blocks = samples.reshape(count, BS, width)

    head, tail, packed = pack(child_map[0, 0], gen_left[0], gen_right[0], blocks)
    low, high = along_front(tail, 1), along_front(head, -1)
    gens = spread_out(packed, ("z", "x"))

    shifted = [around(samples, "col", k) for k in range(1, n_col)]
    local_cols = coupling_cols - lax.axis_index(FRONT) * count + HB
    sparse_range, sparse_rows, up, down = sparse(local_cols, couplings, blocks, low, high)
    shifted, up, down = lax.optimization_barrier((shifted, up, down))
    panels = jnp.stack([samples, *shifted])
    others = around(panels, "half", 1)
    below, above = along_front(up, 1), along_front(down, -1)

    gens, panels, others, sparse_range, sparse_rows = lax.optimization_barrier(
        (gens, panels, others, sparse_range, sparse_rows)
    )
    added = (sparse_range, sparse_rows, below, above)
    partial = reduced(at, gens, panels, others, n_z)
    middle = gens.shape[1] // 2
    first, second = gens[:, :middle], gens[:, middle:]
    up_a, down_b = around(first, "col", 1), around(second, "col", -1)
    up_b, down_a = around(second, "col", 1), around(first, "col", -1)
    far_a, far_b = around(up_a, "col", 1), around(down_b, "col", -1)

    by_z = spread_out(partial, "z")
    by_z = jnp.sum(by_z.astype(F32), axis=0)
    copies = jnp.broadcast_to(by_z, (n_x, *by_z.shape)).reshape(n_x * n_col, *by_z.shape[1:])
    arrived = spread_out(copies, ("x", "col"))
    slice_sum = jnp.sum(arrived.reshape(n_x, n_col, *by_z.shape[1:]), axis=0).astype(BF16)
    copies = jnp.broadcast_to(slice_sum, (n_z, *slice_sum.shape))
    w = spread_out(copies, "z")

    everyone = (gens, up_a, up_b, far_a, far_b, down_a, down_b)
    received = around(low_rank(at, everyone, w), "half", 1)
    range_out, rows_out = (
        (ours + theirs.astype(F32)).astype(BF16)
        for ours, theirs in zip(low_rank(at, everyone, w, added), received)
    )
    return range_out.reshape(samples.shape), rows_out.reshape(samples.shape)


def solution(mesh):
    n_half, n_row, n_col = (mesh.shape[a] for a in ("half", "row", "col"))
    n_x = n_col
    fine = Mesh(
        mesh.devices.reshape(n_half, n_row // n_x, n_x, n_col), ("half", "z", "x", "col")
    )
    row = ("z", "x")
    placed = (
        P(FRONT, "col"),
        P(FRONT, None, None),
        P(FRONT, None),
        P("half", row, None),
        P("half", "col", row),
        P("half", "col", row),
    )
    return jax.shard_map(
        shards,
        mesh=fine,
        in_specs=placed,
        out_specs=(P(FRONT, "col"), P(FRONT, "col")),
        check_vma=False,
    )
```

```python
import functools

import jax
import jax.numpy as jnp
from jax import lax
from jax.experimental import pallas as pl
from jax.experimental.pallas import tpu as pltpu
from jax.sharding import Mesh
from jax.sharding import PartitionSpec as P

BS = 64
NB = 8
HB = 8
LANES = 128
CHUNKS = 1
FRONT = ("half", "z", "x")
F32 = jnp.float32
BF16 = jnp.bfloat16
VMEM = pltpu.VMEM
SMEM = pltpu.SMEM


def whole(space):
    return pl.BlockSpec(memory_space=space)


def cost(flops, moved):
    return pl.CostEstimate(flops=flops, bytes_accessed=moved, transcendentals=0)


def grant(mib, **more):
    return pltpu.CompilerParams(vmem_limit_bytes=mib << 20, **more)


def swapped_halves(x):
    return pltpu.roll(x.astype(F32), BS, 1).astype(BF16)


def low_lanes(shape):
    return lax.broadcasted_iota(jnp.int32, shape, 1) < BS


def pack_kernel(map_ref, left_ref, right_ref, own_ref, head_ref, tail_ref, *out_refs):
    head_ref[...] = own_ref[:HB]
    tail_ref[...] = own_ref[own_ref.shape[0] - HB :]
    ranks = left_ref.shape[0] // len(out_refs)
    low = low_lanes((ranks, LANES))
    for k in range(left_ref.shape[1] // LANES):
        one, two = map_ref[2 * k], map_ref[2 * k + 1]
        for part, out_ref in enumerate(out_refs):
            rows = slice(part * ranks, (part + 1) * ranks)
            left = left_ref[rows, k * LANES : (k + 1) * LANES]
            right = right_ref[rows, k * LANES : (k + 1) * LANES]
            out_ref[one] = jnp.where(low, left, swapped_halves(right))
            out_ref[two] = jnp.where(low, swapped_halves(left), right)


def pack(order_map, left, right, blocks):
    ranks, width = left.shape
    out = jax.ShapeDtypeStruct((width // BS, ranks // CHUNKS, LANES), BF16)
    edge = jax.ShapeDtypeStruct((HB, *blocks.shape[1:]), BF16)
    return pl.pallas_call(
        pack_kernel,
        out_shape=(edge, edge, *(out,) * CHUNKS),
        in_specs=[whole(SMEM)] + [whole(VMEM)] * 3,
        out_specs=(whole(VMEM),) * (2 + CHUNKS),
        cost_estimate=cost(0, 8 * ranks * width),
        name="pack",
    )(order_map, left, right, blocks)


def sparse_kernel(
    cols_ref, a_ref, own_ref, low_ref, high_ref, range_ref, rows_ref, up_ref, down_ref, padded, spread
):
    per = a_ref.shape[0]
    count = own_ref.shape[0]
    step = pl.program_id(0)

    @pl.when(step == 0)
    def _():
        padded[:HB] = low_ref[...]
        padded[HB : HB + count] = own_ref[...]
        padded[HB + count :] = high_ref[...]
        spread[...] = jnp.zeros_like(spread)

    for i in range(per):
        b = step * per + i
        at = [cols_ref[b, t] for t in range(NB)]
        picked = jnp.concatenate([padded[c] for c in at], axis=0)
        a = a_ref[i]
        range_ref[i] = jnp.dot(a, picked, preferred_element_type=F32)
        terms = lax.dot_general(
            a, own_ref[b], (((0,), (0,)), ((), ())), preferred_element_type=F32
        )
        for t in range(NB):
            spread[at[t]] += terms[t * BS : (t + 1) * BS]

    @pl.when(step == pl.num_programs(0) - 1)
    def _():
        rows_ref[...] = spread[HB : HB + count]
        up_ref[...] = spread[HB + count :].astype(BF16)
        down_ref[...] = spread[:HB].astype(BF16)


def sparse(local_cols, couplings, blocks, low, high):
    count, _, width = blocks.shape
    per = 8
    edge = jax.ShapeDtypeStruct((HB, BS, width), BF16)
    return pl.pallas_call(
        sparse_kernel,
        grid=(count // per,),
        out_shape=(
            jax.ShapeDtypeStruct((count, BS, width), F32),
            jax.ShapeDtypeStruct((count, BS, width), F32),
            edge,
            edge,
        ),
        in_specs=[
            whole(SMEM),
            pl.BlockSpec((per, BS, NB * BS), lambda i: (i, 0, 0)),
            whole(VMEM),
            whole(VMEM),
            whole(VMEM),
        ],
        out_specs=(
            pl.BlockSpec((per, BS, width), lambda i: (i, 0, 0)),
            whole(VMEM),
            whole(VMEM),
            whole(VMEM),
        ),
        scratch_shapes=[
            pltpu.VMEM((count + 2 * HB, BS, width), BF16),
            pltpu.VMEM((count + 2 * HB, BS, width), F32),
        ],
        compiler_params=grant(12, dimension_semantics=("arbitrary",)),
        cost_estimate=cost(4 * count * BS * BS * NB * width, 6 << 20),
        name="sparse",
    )(local_cols, couplings, blocks, low, high)


def reduce_kernel(at_ref, gen_ref, own_ref, other_ref, out_ref, lhs):
    half, me = at_ref[0], at_ref[1]
    blocks, ranks, _ = gen_ref.shape
    count = blocks // 2
    parts = own_ref.shape[0]
    low = low_lanes((ranks, LANES))
    for side, first in ((0, half * count), (1, (1 - half) * count)):
        for k in range(count // 2):
            one, two = gen_ref[first + 2 * k], gen_ref[first + 2 * k + 1]
            lanes = slice(k * LANES, (k + 1) * LANES)
            lhs[side, :ranks, lanes] = jnp.where(low, one, swapped_halves(two))
            lhs[side, ranks:, lanes] = jnp.where(low, swapped_halves(one), two)
    for pair in range(0, parts, 2):
        total = 0.0
        for side, ref in ((0, own_ref), (1, other_ref)):
            rhs = jnp.concatenate([ref[pair], ref[pair + 1]], axis=1)
            total += jnp.dot(lhs[side], rhs, preferred_element_type=F32)
        for k in range(2):
            piece = total[:, k * LANES : (k + 1) * LANES]
            slot = lax.rem(me + parts - (pair + k), parts)
            out_ref[:, slot] = piece.reshape(out_ref.shape[0], -1, LANES).astype(BF16)


def reduced(at, gens, own, other, splits):
    _, ranks, _ = gens.shape
    parts, rows, _ = own.shape
    out = jax.ShapeDtypeStruct((splits, parts, 2 * ranks // splits, LANES), BF16)
    return pl.pallas_call(
        reduce_kernel,
        out_shape=out,
        in_specs=[whole(SMEM)] + [whole(VMEM)] * 3,
        out_specs=whole(VMEM),
        scratch_shapes=[pltpu.VMEM((2, 2 * ranks, rows), BF16)],
        compiler_params=grant(14),
        cost_estimate=cost(8 * ranks * rows * parts * LANES, 6 << 20),
        name="partials",
    )(at, gens, own, other)


def low_rank_kernel(mine, pieces, at_ref, *refs):
    gens, w_ref, refs = refs[:pieces], refs[pieces], refs[pieces + 1 :]
    me, step, steps = at_ref[1], pl.program_id(0), pl.num_programs(0)
    per, ranks, _ = gens[0].shape
    lhs = refs[-1]
    parts = lhs.shape[1] // ranks
    low = low_lanes((LANES, LANES))

    @pl.when(step == 0)
    def _():
        for k in range(parts):
            both = w_ref[:, lax.rem(me + parts - k, parts)].reshape(2 * ranks, LANES)
            turned = both.astype(F32).T.astype(BF16)
            lanes = slice(k * ranks, (k + 1) * ranks)
            lhs[:LANES, lanes] = turned[:, ranks:]
            lhs[LANES:, lanes] = turned[:, :ranks]

    for i in range(0, per, 2):
        rhs = jnp.concatenate(
            [jnp.concatenate([g[i + j] for g in gens], axis=0) for j in range(2)], axis=1
        )
        both = jnp.dot(lhs[...], rhs, preferred_element_type=F32)
        for j in range(2):
            lanes = slice(j * LANES, (j + 1) * LANES)
            out = jnp.where(low, both[:LANES, lanes], both[LANES:, lanes]).T
            for_range, for_rows = out[:BS], out[BS:]
            b = i + j
            if mine:
                sr_ref, sp_ref, below_ref, above_ref, range_ref, rows_ref = refs[:-1]
                range_ref[b] = for_range + sr_ref[b]
                for_rows += sp_ref[b]
                if b < HB:
                    for_rows += jnp.where(step == 0, below_ref[b].astype(F32), 0.0)
                if b >= per - HB:
                    above = above_ref[b - (per - HB)].astype(F32)
                    for_rows += jnp.where(step == steps - 1, above, 0.0)
                rows_ref[b] = for_rows
            else:
                refs[0][0, b] = for_range.astype(BF16)
                refs[0][1, b] = for_rows.astype(BF16)


def low_rank(at, gens, w, added=()):
    blocks, _, _ = gens[0].shape
    count, per = blocks // 2, 2 * HB
    steps = count // per
    mine = bool(added)
    depth = sum(g.shape[1] for g in gens)

    def place(i, at_ref):
        half = at_ref[0] if mine else 1 - at_ref[0]
        return (half * steps + i, 0, 0)

    def tiles(rows):
        return pl.BlockSpec((per, rows, LANES), place)

    flat = pl.BlockSpec((per, BS, LANES), lambda i, at_ref: (i, 0, 0))
    edges = [flat] * 2 + [whole(VMEM)] * 2
    if mine:
        out_shape = (jax.ShapeDtypeStruct((count, BS, LANES), F32),) * 2
        out_specs = (flat, flat)
    else:
        out_shape = jax.ShapeDtypeStruct((2, count, BS, LANES), BF16)
        out_specs = pl.BlockSpec((2, per, BS, LANES), lambda i, at_ref: (0, i, 0, 0))
    return pl.pallas_call(
        functools.partial(low_rank_kernel, mine, len(gens)),
        grid_spec=pltpu.PrefetchScalarGridSpec(
            num_scalar_prefetch=1,
            grid=(steps,),
            in_specs=[tiles(g.shape[1]) for g in gens] + [whole(VMEM)] + (edges if mine else []),
            out_specs=out_specs,
            scratch_shapes=[pltpu.VMEM((2 * LANES, depth), BF16)],
        ),
        out_shape=out_shape,
        compiler_params=grant(10, dimension_semantics=("arbitrary",)),
        cost_estimate=cost(4 * count * LANES * depth * LANES, 4 << 20),
        name="mine" if mine else "theirs",
    )(at, *gens, w, *added)


def around(x, axis, by):
    count = lax.axis_size(axis)
    return lax.ppermute(x, axis, [(i, (i + by) % count) for i in range(count)])


def along_front(x, by):
    count = lax.axis_size(FRONT)
    pairs = [(i, i + by) for i in range(count) if 0 <= i + by < count]
    return lax.ppermute(x, FRONT, pairs)


def spread_out(x, axis):
    return lax.all_to_all(x, axis, split_axis=0, concat_axis=0, tiled=True)


def shards(samples, couplings, coupling_cols, child_map, gen_left, gen_right):
    count = couplings.shape[0]
    width = samples.shape[1]
    half, me = lax.axis_index("half"), lax.axis_index("col")
    at = jnp.stack([half, me]).astype(jnp.int32)
    n_z, n_x, n_col = (lax.axis_size(a) for a in ("z", "x", "col"))
    blocks = samples.reshape(count, BS, width)

    head, tail, packed = pack(child_map[0, 0], gen_left[0], gen_right[0], blocks)
    low, high = along_front(tail, 1), along_front(head, -1)
    gens = spread_out(packed, ("z", "x"))

    shifted = [around(samples, "col", k) for k in range(1, n_col)]
    local_cols = coupling_cols - lax.axis_index(FRONT) * count + HB
    sparse_range, sparse_rows, up, down = sparse(local_cols, couplings, blocks, low, high)
    shifted, up, down = lax.optimization_barrier((shifted, up, down))
    panels = jnp.stack([samples, *shifted])
    others = around(panels, "half", 1)
    below, above = along_front(up, 1), along_front(down, -1)

    gens, panels, others, sparse_range, sparse_rows = lax.optimization_barrier(
        (gens, panels, others, sparse_range, sparse_rows)
    )
    added = (sparse_range, sparse_rows, below, above)
    partial = reduced(at, gens, panels, others, n_z)
    middle = gens.shape[1] // 2
    first, second = gens[:, :middle], gens[:, middle:]
    up_a, down_b = around(first, "col", 1), around(second, "col", -1)
    up_b, down_a = around(second, "col", 1), around(first, "col", -1)
    far_a, far_b = around(up_a, "col", 1), around(down_b, "col", -1)

    by_z = spread_out(partial, "z")
    by_z = jnp.sum(by_z.astype(F32), axis=0)
    copies = jnp.broadcast_to(by_z, (n_x, *by_z.shape)).reshape(n_x * n_col, *by_z.shape[1:])
    arrived = spread_out(copies, ("x", "col"))
    slice_sum = jnp.sum(arrived.reshape(n_x, n_col, *by_z.shape[1:]), axis=0).astype(BF16)
    copies = jnp.broadcast_to(slice_sum, (n_z, *slice_sum.shape))
    w = spread_out(copies, "z")

    everyone = (gens, up_a, up_b, far_a, far_b, down_a, down_b)
    received = around(low_rank(at, everyone, w), "half", 1)
    range_out, rows_out = (
        (ours + theirs.astype(F32)).astype(BF16)
        for ours, theirs in zip(low_rank(at, everyone, w, added), received)
    )
    return range_out.reshape(samples.shape), rows_out.reshape(samples.shape)


def solution(mesh):
    n_half, n_row, n_col = (mesh.shape[a] for a in ("half", "row", "col"))
    n_x = n_col
    fine = Mesh(
        mesh.devices.reshape(n_half, n_row // n_x, n_x, n_col), ("half", "z", "x", "col")
    )
    row = ("z", "x")
    placed = (
        P(FRONT, "col"),
        P(FRONT, None, None),
        P(FRONT, None),
        P("half", row, None),
        P("half", "col", row),
        P("half", "col", row),
    )
    return jax.shard_map(
        shards,
        mesh=fine,
        in_specs=placed,
        out_specs=(P(FRONT, "col"), P(FRONT, "col")),
        check_vma=False,
    )
```
